32 devices in a mesh: gx: 8 (over y, x, core), gy: 4 (over z).
Axes of the slice: x: 2, y: 2, z: 4, core: 2. Of those that a mesh axis runs over, the one named last changes fastest.
Arguments:
- tokens: bfloat16 [4096, 2048], P(('gx', 'gy')), may hold values from -6 to 6
- expert_ids: int32 [4096, 8], P(('gx', 'gy')), may hold values from 0 to 31, all different within a row; in each aligned block of 128 rows (0 to 127, 128 to 255, ...) at most 96 rows name the same one
- w_gate: bfloat16 [32, 2048, 768], P(('gx', 'gy')), may hold values from -0.125 to 0.125
- w_up: bfloat16 [32, 2048, 768], P(('gx', 'gy')), may hold values from -0.125 to 0.125
- down_error: float32 [32, 768, 2048], P(('gx', 'gy')), may hold values from -18 to 18
Outputs:
- gram_error: float32 [32, 768, 2048], P(('gx', 'gy'))
The draws below stay inside these ranges and needn't reach their ends.
Inputs may be any that keep to these rules, and one draw needn't show every extreme that they name: `expert_ids`: among the rows of one device no expert is named more than 96 times, a bound that some block reaches; every expert is named by some row; the 8 ids of a row are distinct.
All inputs are finite; a program needn't handle non-finite values.
Results may differ from the reference program's by a relative error of at most 0.0036.
Values may be sent and summed in bfloat16 or wider, within the bound.
A program may use at most 128 MiB of HBM per device.

```python
import math
import jax
import jax.numpy as jnp
import numpy as np
from jax import lax

D = 2048
FF = 768
TOP = 8
TOK_DEV = 128
EXPERTS = 32
TOKENS = 4096
CAP = 96


def shard_levels(stream_key, dims, pieces, low, top_value):
    def one(position, blocks):
        heights = jax.random.uniform(jax.random.fold_in(jax.random.fold_in(stream_key, 6), position), (blocks,), jnp.float32, low / len(pieces), top_value / len(pieces))
        return jnp.repeat(jnp.exp(heights), dims[position] // blocks).reshape((-1,) + (1,) * (len(dims) - position - 1))

    factor_of = one(*pieces[0])
    for cut in pieces[1:]:
        factor_of = factor_of * one(*cut)
    return factor_of


def shared_out(own_key, own, number, rows, count, top, limit, skew):
    sequence = jax.random.permutation(own_key, count)
    packed, ordinary = portions_of(count, rows * top, limit, skew, True), portions_of(count, rows * top, limit, skew, False)
    places = jnp.arange(count)

    def named(sizes, offset_by):
        used = int((sizes > 0).sum())
        fixed = max(1, used // 4)
        shifted = fixed + (places - fixed + offset_by * (used - fixed)) % max(1, count - fixed)
        return jnp.zeros((count,), jnp.int32).at[sequence[jnp.where(places < fixed, places, shifted)]].set(jnp.asarray(sizes, jnp.int32))

    sizes = jnp.where(number % 4 == 0, named(packed, number // 4), named(ordinary, number - number // 4 - 1))
    mixed = jax.random.permutation(jax.random.fold_in(own, 3), count)
    source_of, sink = mixed[0:count // 2 * 2:2], mixed[1:count // 2 * 2:2]
    room = jnp.minimum(sizes[source_of] - 1, limit - sizes[sink]) // 2
    room = jnp.where((source_of == sequence[0]) | (sink == sequence[0]) | (sizes[sink] == 0), 0, jnp.maximum(room, 0))
    shifted = jax.random.randint(jax.random.fold_in(own, 4), (count // 2,), 0, 1 << 20) % (room + 1)
    sizes = sizes.at[source_of].add(-shifted).at[sink].add(shifted)
    items = jnp.searchsorted(jnp.cumsum(sizes), jnp.arange(rows * top), side="right").astype(jnp.int32)
    table = items.reshape(top, rows).T
    table = table[jax.random.permutation(jax.random.fold_in(own, 1), rows)]
    offset_by = jax.random.randint(jax.random.fold_in(own, 2), (rows, 1), 0, top)
    return jnp.take_along_axis(table, (jnp.arange(top)[None, :] + offset_by) % top, axis=1)


def portions_of(number_of, total, limit, lean, full):
    weights = [(1 << 20) // math.isqrt(grade ** lean) + 1 for grade in range(1, number_of + 1)]
    largest = limit if full else min(limit, max(-(-total // number_of), total * weights[0] // sum(weights)))
    least = 1 if total - largest >= number_of - 1 else 0
    holding, rest = [largest] + [least] * (number_of - 1), total - largest - least * (number_of - 1)
    while rest > 0:
        movable = [i for i in range(1, number_of) if holding[i] < largest] or [i for i in range(1, number_of) if holding[i] < limit]
        mass, remaining = sum([weights[i] for i in movable]), rest
        for i in movable:
            extra = min(limit - holding[i], max(1, remaining * weights[i] // mass), rest)
            holding[i] = holding[i] + extra
            rest = rest - extra
    return np.array(holding)


def normal_values(stream_key, shape, scale, bound, shards=(), kind=jnp.bfloat16):
    factor_of = shard_levels(stream_key, shape, shards, -0.22, 0.18) if shards else 1.0
    drawn = jax.random.normal(stream_key, shape, jnp.float32) * scale * factor_of
    return jnp.minimum(jnp.maximum(drawn, -bound), bound).astype(kind)


def setup_inputs(seed: int = 0) -> dict:
    splits = jax.random.split(jax.random.key(seed), 6)
    tokens = normal_values(splits[0], (TOKENS, D), 1.0, 6.0, ((0, 32),))
    expert_ids_keys = jax.random.split(jax.random.fold_in(splits[1], 1), TOKENS // TOK_DEV)
    expert_ids_turns = jax.random.permutation(jax.random.fold_in(splits[1], 3), TOKENS // TOK_DEV)
    expert_ids = jax.vmap(lambda own, number: shared_out(jax.random.fold_in(splits[1], 2), own, number, TOK_DEV, EXPERTS, TOP, CAP, 2))(expert_ids_keys, expert_ids_turns).reshape((TOKENS, TOP))
    w_gate = normal_values(splits[2], (EXPERTS, D, FF), D ** -0.5, 0.125, ((0, 32),))
    w_up = normal_values(splits[3], (EXPERTS, D, FF), D ** -0.5, 0.125, ((0, 32),))
    down_error = normal_values(splits[4], (EXPERTS, FF, D), 3.0, 18.0, ((0, 32),), jnp.float32)
    return dict(tokens=tokens, expert_ids=expert_ids, w_gate=w_gate, w_up=w_up, down_error=down_error)


def reference(tokens, expert_ids, w_gate, w_up, down_error):
    flat_ids = expert_ids.reshape(-1).astype(jnp.int32)
    total = flat_ids.shape[0]
    block_rows = 256
    ordering = jnp.argsort(flat_ids, stable=True).astype(jnp.int32)
    padded_order = jnp.concatenate([ordering, jnp.zeros((block_rows,), jnp.int32)])
    counts = jnp.sum((flat_ids[:, None] == jnp.arange(EXPERTS, dtype=jnp.int32)[None, :]).astype(jnp.int32), axis=0)
    starts = (jnp.cumsum(counts) - counts).astype(jnp.int32)

    def one_expert(expert):
        start = starts[expert]
        count = counts[expert]
        gate_matrix = w_gate[expert]
        up_matrix = w_up[expert]

        def add_block(number, accum):
            offset = (number * block_rows).astype(jnp.int32)
            window = lax.dynamic_slice(padded_order, (start + offset,), (block_rows,))
            live = (offset + jnp.arange(block_rows, dtype=jnp.int32)) < count
            picked = tokens[window // TOP]
            gate = jnp.dot(picked, gate_matrix, preferred_element_type=jnp.float32)
            upward = jnp.dot(picked, up_matrix, preferred_element_type=jnp.float32)
            hidden = jnp.where(live[:, None], jax.nn.silu(gate) * upward, jnp.zeros_like(gate)).astype(jnp.bfloat16)
            return accum + jnp.dot(hidden.T, hidden, preferred_element_type=jnp.float32)

        blocks = ((count + block_rows - 1) // block_rows).astype(jnp.int32)
        gram = lax.fori_loop(jnp.int32(0), blocks, add_block, jnp.zeros((FF, FF), jnp.float32))
        mean_gram = gram / count.astype(jnp.float32)
        return jnp.dot(mean_gram, down_error[expert], preferred_element_type=jnp.float32, precision=lax.Precision.HIGHEST)

    return lax.map(one_expert, jnp.arange(EXPERTS, dtype=jnp.int32))
```

```python
import jax
import jax.numpy as jnp
from jax import lax
from jax.experimental import pallas as pl
from jax.experimental.pallas import tpu as pltpu
from jax.sharding import PartitionSpec as P

MESH = pl.DeviceIdType.MESH
LANES = 128
VMEM_LIMIT = 59572224
FINISH_LIMIT = 16 * 1024 * 1024


STEPS = 10
CORNER, MIDDLE = 0, 1
FIRST = (0, 3, 5, 7)
FINISH_COLS = 256


def place(role, j, k, h):
    if j == 1:
        return FIRST[k] + 1 - h, 0
    if j == 2:
        return FIRST[k] + h, 1
    if j == 3 and k == 0:
        return 2, h
    if role == CORNER:
        if j == 3 and k == 3:
            return 9, h
        first = {(0, 1): 0, (0, 2): 2, (0, 3): 4, (3, 1): 6, (3, 2): 8}[j, k]
        return first + h, 2
    if j == 0 and k == 1:
        return (8, 2) if h == 0 else (9, 0)
    if j == 3 and k == 1:
        return 9, 1 + h
    first = {(0, 2): 0, (0, 3): 2, (3, 2): 4, (3, 3): 6}[j, k]
    return first + h, 2


def arrival(role, j, k, h):
    if role == MIDDLE and k == 1 and j in (0, 3):
        return h if j == 0 else 4 + h
    return place(role, j, k, h)[0]


def blocks():
    return [(j, k) for j in range(4) for k in range(4) if (j, k) != (0, 0)]


def arrivals(role, step):
    halves = [(j, k, h) for j, k in blocks() for h in range(2) if arrival(role, j, k, h) == step]
    ids = [(j, k) for j, k in blocks() if min(arrival(role, j, k, h) for h in range(2)) == step]
    return halves, ids


def sends(role, step):
    out = []

    def put(queue, block, halves, there, ids=True):
        if ids:
            out.append((queue, block, None, there))
        out.extend((queue, block, h, there) for h in halves)

    if step < 0:
        put("x", (0, 0), (1, 0), (1, 0))
        put("y", (0, 0), (0, 1), (2, 0))
        put("in", (0, 0), (0, 1), (0, 1) if role == CORNER else (0, 2))
        if role == MIDDLE:
            put("out", (0, 0), (0, 1), (0, 1))
    if step == 0:
        put("x", (2, 0), (0,), (3, 0))
        put("y", (1, 0), (1,), (3, 0), ids=False)
    columns = {1: (1,), 3: (2,), 5: (3,)} if role == CORNER else {1: (1, 2), 3: (3,)}
    for k in columns.get(step, ()):
        put("x", (0, k), (1, 0), (1, k))
        put("y", (0, k), (0, 1), (2, k))
    if role == CORNER:
        if step == 2:
            put("in", (3, 0), (0, 1), (3, 1))
        if step == 7:
            put("x", (2, 3), (0,), (3, 3))
            put("y", (1, 3), (1,), (3, 3), ids=False)
        return out
    if step in (0, 1):
        put("out", (0, 2), (step,), (0, 2), ids=step == 0)
        put("in", (0, 1), (step,), (0, 3), ids=step == 0)
    if step == 2:
        put("out", (0, 3), (0,), (0, 3))
        put("in", (3, 0), (0, 1), (3, 2))
    if step == 3:
        put("out", (0, 3), (1,), (0, 3), ids=False)
        put("out", (3, 0), (0, 1), (3, 1))
    if step in (4, 5):
        put("out", (3, 2), (step - 4,), (3, 2), ids=step == 4)
        put("in", (3, 1), (step - 4,), (3, 3), ids=step == 4)
    return out


def receiver(role, queue):
    if queue in ("x", "y"):
        return role
    return CORNER if queue == "out" else MIDDLE


def packed_tables():
    words = []
    for role in (CORNER, MIDDLE):
        held = {place(role, j, k, h): (j * 4 + k) * 2 + h for j, k in blocks() for h in range(2)}
        words.append([
            [sum(held[s, link] << (5 * (s % 6)) for s in range(first, min(first + 6, STEPS))) for first in (0, 6)]
            for link in range(3)
        ])
    return words


def gather_kernel(
    x_hbm, ids_hbm, wg_hbm, wu_hbm, out_ref,
    own, tok, idb, wg, wu, hid, acc, turned, mask,
    s_send, s_recv, s_idr, s_pair, s_part, s_load,
):
    gx = lax.axis_index("gx")
    z = lax.axis_index("gy")
    rows, width = x_hbm.shape
    half = rows // 2
    lot = 3 * rows
    core = gx % 2
    px = (gx // 2) % 2
    py = gx // 4
    expert = gx * 4 + z
    mirror = z // 2
    inner = z + (3 - 2 * z) * mirror

    def dev(a, b, c):
        return b * 4 + a * 2 + c

    inward = z + 1 - 2 * mirror
    target = {
        "x": (dev(1 - px, py, core), z),
        "y": (dev(px, 1 - py, core), z),
        "in": (gx, inward),
        "out": (gx, z - 1 + 2 * mirror),
        "pair": (dev(px, py, 1 - core), z),
    }

    def remote(src, dst, ssem, rsem, to):
        return pltpu.make_async_remote_copy(
            src_ref=src, dst_ref=dst, send_sem=ssem, recv_sem=rsem,
            device_id=target[to], device_id_type=MESH,
        )

    def spot(s, link, c):
        return tok.at[s, pl.ds((link * 2 + c) * half, half), :]

    def number(j, k):
        return j * 4 + k

    order = {}
    for role in (CORNER, MIDDLE):
        n = 0
        for step in range(-1, STEPS):
            for item in sends(role, step):
                order[role, item] = n
                n += 1

    def send_copy(role, item):
        queue, (j, k), h, there = item
        far = receiver(role, queue)
        ssem = s_send.at[order[role, item]]
        if h is None:
            src = ids_hbm if (j, k) == (0, 0) else idb.at[number(j, k), core]
            return remote(src, idb.at[number(*there), core], ssem, s_idr.at[number(*there)], queue)
        src = x_hbm.at[pl.ds(h * half, half), :] if (j, k) == (0, 0) else spot(*place(role, j, k, h), core)
        s, link = place(far, *there, h)
        return remote(src, spot(s, link, core), ssem, s_recv.at[s, link], queue)

    def pair_piece(s, link):
        return remote(spot(s, link, core), spot(s, link, core), s_pair.at[s * 3 + link], s_part.at[s * 3 + link], "pair")

    def pair_ids(b):
        n = 3 * STEPS + b
        src = ids_hbm if b == 0 else idb.at[b, core]
        return remote(src, idb.at[b, core], s_pair.at[n], s_part.at[n], "pair")

    n_own = 3 * STEPS + 16
    pair_own = remote(x_hbm, own.at[pl.ds(core * rows, rows), :], s_pair.at[n_own], s_part.at[n_own], "pair")

    def wait_piece(s, link):
        remote(spot(s, link, core), spot(s, link, core), s_send.at[0], s_recv.at[s, link], "pair").wait_recv()

    def wait_ids(b):
        remote(idb.at[b, core], idb.at[b, core], s_send.at[0], s_idr.at[b], "pair").wait_recv()

    def wait_pair_piece(s, link):
        n = s * 3 + link
        remote(spot(s, link, 1 - core), spot(s, link, 1 - core), s_send.at[0], s_part.at[n], "pair").wait_recv()

    def wait_pair_ids(b):
        n = 3 * STEPS + b
        remote(idb.at[b, 1 - core], idb.at[b, 1 - core], s_send.at[0], s_part.at[n], "pair").wait_recv()

    bands = 3
    features = hid.shape[1]
    band = features // bands

    def turn(b, c):
        hits = jnp.sum((idb[b, c] == expert).astype(jnp.float32), axis=0, keepdims=True)
        return jnp.broadcast_to(hits, (LANES, rows)).T

    def hidden(rows_in, count, base):
        live = jnp.concatenate([mask[pl.ds(0, count), :]] * (band // LANES), axis=1)
        for n in range(bands):
            cols = pl.ds(n * band, band)
            gate = jnp.dot(rows_in, wg[:, cols], preferred_element_type=jnp.float32)
            upward = jnp.dot(rows_in, wu[:, cols], preferred_element_type=jnp.float32)
            value = gate / (1.0 + jnp.exp(-gate)) * upward
            hid[pl.ds(base, count), cols] = jnp.where(live > 0.5, value, 0.0).astype(jnp.bfloat16)

    def gram(count, start):
        for n in range(bands):
            rest = pl.ds(n * band, features - n * band)
            part = lax.dot_general(
                hid[pl.ds(0, count), pl.ds(n * band, band)], hid[pl.ds(0, count), rest],
                (((0,), (0,)), ((), ())), preferred_element_type=jnp.float32,
            )
            if start:
                acc[pl.ds(n * band, band), rest] = part
            else:
                acc[pl.ds(n * band, band), rest] += part

    tables = packed_tables()

    def entry(link, s):
        corner, middle = tables[CORNER][link], tables[MIDDLE][link]
        low = corner[0] + (middle[0] - corner[0]) * inner
        high = corner[1] + (middle[1] - corner[1]) * inner
        word = low + (high - low) * (s // 6)
        return (word >> (5 * (s % 6))) % 32

    def unit(s):
        for link in range(3):
            held = entry(link, s)
            b, h = held // 2, held % 2
            for c in range(2):
                turned[link * 2 + c] = turn(b, c)
                mask[pl.ds((link * 2 + c) * half, half), :] = turned[link * 2 + c, pl.ds(pl.multiple_of(h * half, half), half), :]
        hidden(tok[s], lot, pl.multiple_of((s % 2) * lot, lot))

    barrier = pltpu.get_barrier_semaphore()
    for to in ("x", "y", "in", "pair"):
        pl.semaphore_signal(barrier, inc=1, device_id=target[to], device_id_type=MESH)

    @pl.when(inner == 1)
    def _():
        pl.semaphore_signal(barrier, inc=1, device_id=target["out"], device_id_type=MESH)

    local = pltpu.make_async_copy(x_hbm, own.at[pl.ds(core * rows, rows), :], s_load.at[0])
    local_ids = pltpu.make_async_copy(ids_hbm, idb.at[0, core], s_load.at[1])
    load_g = pltpu.make_async_copy(wg_hbm, wg, s_load.at[2])
    load_u = pltpu.make_async_copy(wu_hbm, wu, s_load.at[3])
    local.start()
    local_ids.start()
    load_g.start()
    load_u.start()
    pl.semaphore_wait(barrier, 4 + inner)

    roles = ((CORNER, inner == 0), (MIDDLE, inner == 1))
    for role, here in roles:
        @pl.when(here)
        def _():
            for item in sends(role, -1):
                send_copy(role, item).start()

    pair_ids(0).start()
    pair_own.start()
    local.wait()
    local_ids.wait()
    wait_pair_ids(0)
    theirs = own.at[pl.ds((1 - core) * rows, rows), :]
    remote(theirs, theirs, s_send.at[0], s_part.at[n_own], "pair").wait_recv()
    load_g.wait()
    load_u.wait()
    for c in range(2):
        mask[pl.ds(c * rows, rows), :] = turn(0, c)
    hidden(own[...], 2 * rows, 0)
    gram(2 * rows, True)

    def drain(role, step):
        for item in sends(role, step):
            send_copy(role, item).wait_send()
        if step < 0:
            pair_ids(0).wait_send()
            pair_own.wait_send()
            return
        halves, ids = arrivals(role, step)
        for j, k in ids:
            pair_ids(number(j, k)).wait_send()
        for j, k, h in halves:
            pair_piece(*place(role, j, k, h)).wait_send()

    late = 5

    def loop(s, carry):
        for role, here in roles:
            for step in range(STEPS + 1):
                @pl.when(jnp.logical_and(here, s == step))
                def _():
                    if step < STEPS:
                        halves, ids = arrivals(role, step)
                        for j, k in ids:
                            wait_ids(number(j, k))
                        for j, k, h in halves:
                            wait_piece(*place(role, j, k, h))
                        for item in sends(role, step):
                            send_copy(role, item).start()
                        for j, k in ids:
                            pair_ids(number(j, k)).start()
                        for j, k, h in halves:
                            pair_piece(*place(role, j, k, h)).start()
                    if step >= late - 1:
                        drain(role, step - late)
                    if step:
                        halves, ids = arrivals(role, step - 1)
                        for j, k in ids:
                            wait_pair_ids(number(j, k))
                        for j, k, h in halves:
                            wait_pair_piece(*place(role, j, k, h))

        @pl.when(s > 0)
        def _():
            unit(s - 1)

        @pl.when(jnp.logical_and(s > 0, s % 2 == 0))
        def _():
            gram(2 * lot, False)

        return carry

    lax.fori_loop(0, STEPS + 1, loop, 0)
    count = jnp.sum((idb[...] == expert).astype(jnp.float32))
    for n in range(bands):
        for m in range(n, bands):
            part = acc[pl.ds(n * band, band), pl.ds(m * band, band)] / count
            out_ref[pl.ds(n * band, band), pl.ds(m * band, band)] = part.astype(out_ref.dtype)
            if m > n:
                out_ref[pl.ds(m * band, band), pl.ds(n * band, band)] = part.T.astype(out_ref.dtype)
    for role, here in roles:
        @pl.when(here)
        def _():
            for step in range(STEPS + 1 - late, STEPS):
                drain(role, step)


def finish_kernel(gram_ref, error_ref, out_hbm, done, sem):
    cols = done.shape[2]
    turns = error_ref.shape[1] // cols

    def put(n):
        return pltpu.make_async_copy(done.at[n % 2], out_hbm.at[:, pl.ds(n * cols, cols)], sem.at[n % 2])

    for n in range(turns):
        if n >= 2:
            put(n - 2).wait()
        done[n % 2] = jnp.dot(
            gram_ref[...], error_ref[:, pl.ds(n * cols, cols)].astype(jnp.bfloat16),
            preferred_element_type=jnp.float32,
        )
        put(n).start()
    for n in range(turns - 2, turns):
        put(n).wait()


def fused_local(tokens, expert_ids, w_gate, w_up, down_error):
    rows, width = tokens.shape
    top = expert_ids.shape[1]
    features = w_gate.shape[2]
    vmem = pl.BlockSpec(memory_space=pltpu.VMEM)
    hbm = pl.BlockSpec(memory_space=pltpu.HBM)
    dma = pltpu.SemaphoreType.DMA
    n_sends = max(sum(len(sends(role, step)) for step in range(-1, STEPS)) for role in (CORNER, MIDDLE))
    pieces = 3 * STEPS + 17
    mean_gram = pl.pallas_call(
        gather_kernel,
        out_shape=jax.ShapeDtypeStruct((features, features), jnp.bfloat16),
        in_specs=[hbm] * 4,
        out_specs=vmem,
        scratch_shapes=[
            pltpu.VMEM((2 * rows, width), jnp.bfloat16),
            pltpu.VMEM((STEPS, 3 * rows, width), jnp.bfloat16),
            pltpu.VMEM((16, 2, top, rows), jnp.int32),
            pltpu.VMEM((width, features), jnp.bfloat16),
            pltpu.VMEM((width, features), jnp.bfloat16),
            pltpu.VMEM((6 * rows, features), jnp.bfloat16),
            pltpu.VMEM((features, features), jnp.float32),
            pltpu.VMEM((6, rows, LANES), jnp.float32),
            pltpu.VMEM((3 * rows, LANES), jnp.float32),
            dma((n_sends,)), dma((STEPS, 3)), dma((16,)), dma((pieces,)), dma((pieces,)), dma((4,)),
        ],
        compiler_params=pltpu.CompilerParams(
            collective_id=0, has_side_effects=True, vmem_limit_bytes=VMEM_LIMIT
        ),
    )(tokens, expert_ids.T, w_gate[0], w_up[0])
    return pl.pallas_call(
        finish_kernel,
        out_shape=jax.ShapeDtypeStruct(down_error.shape[1:], jnp.float32),
        in_specs=[vmem, vmem],
        out_specs=hbm,
        scratch_shapes=[pltpu.VMEM((2, features, FINISH_COLS), jnp.float32), dma((2,))],
        compiler_params=pltpu.CompilerParams(vmem_limit_bytes=FINISH_LIMIT),
    )(mean_gram, down_error[0])[None]


def hidden_rows(received, w_gate, w_up):
    sources, slots, width = received.shape
    flat_rows = received.reshape(sources * slots, width)
    gate = jnp.dot(flat_rows, w_gate[0], preferred_element_type=jnp.float32)
    upward = jnp.dot(flat_rows, w_up[0], preferred_element_type=jnp.float32)
    hidden = (jax.nn.silu(gate) * upward).astype(jnp.bfloat16)
    return hidden.reshape(sources, slots, hidden.shape[1])


def cross_gram(first, second):
    return lax.dot_general(
        first, second, (((0,), (0,)), ((), ())), preferred_element_type=jnp.float32
    )


def gram_of(hidden):
    middle = hidden.shape[1] // 2
    left_part = hidden[:, :middle]
    right_part = hidden[:, middle:]
    upper_left = cross_gram(left_part, left_part)
    upper_right = cross_gram(left_part, right_part)
    lower_right = cross_gram(right_part, right_part)
    top_band = jnp.concatenate([upper_left, upper_right], axis=1)
    bottom_band = jnp.concatenate([upper_right.T, lower_right], axis=1)
    return jnp.concatenate([top_band, bottom_band], axis=0)


def local(tokens, expert_ids, w_gate, w_up, down_error):
    across = lax.axis_size("gx")
    within = lax.axis_size("gy")
    experts = across * within
    tok_count, top_count = expert_ids.shape
    width = tokens.shape[1]
    assigned = tok_count * top_count
    capacity = 3 * assigned // experts
    flat_ids = expert_ids.reshape(assigned)
    onehot = (flat_ids[:, None] == jnp.arange(experts, dtype=jnp.int32)[None, :]).astype(
        jnp.bfloat16
    )
    positions = jnp.arange(assigned, dtype=jnp.int32)
    lower = (positions[:, None] >= positions[None, :]).astype(jnp.bfloat16)
    running = jnp.dot(lower, onehot, preferred_element_type=jnp.float32)
    slot_of = (jnp.sum(running * onehot, axis=1) - 1.0).astype(jnp.int32)
    target = flat_ids * capacity + slot_of
    picked = tokens[positions // top_count]
    outgoing = jnp.zeros((experts * capacity, width), jnp.bfloat16).at[target].set(picked)
    tallies = jnp.sum(onehot.astype(jnp.float32), axis=0)
    loads = lax.psum_scatter(tallies, ("gx", "gy"), scatter_dimension=0, tiled=True)
    hidden = hidden_rows(
        lax.all_to_all(
            outgoing.reshape(experts, capacity, width),
            ("gx", "gy"),
            split_axis=0,
            concat_axis=0,
            tiled=True,
        ),
        w_gate,
        w_up,
    )
    hidden = hidden.reshape(experts * capacity, hidden.shape[2])
    gram = gram_of(hidden)
    mean_gram = gram / loads[0]
    product = jnp.dot(
        mean_gram,
        down_error[0],
        preferred_element_type=jnp.float32,
        precision=lax.Precision.HIGHEST,
    )
    return product[None]


def solution(mesh):
    small = mesh.shape["gx"] == 8 and mesh.shape["gy"] == 4
    return jax.shard_map(
        fused_local if small else local,
        mesh=mesh,
        in_specs=(
            P(("gx", "gy"), None),
            P(("gx", "gy"), None),
            P(("gx", "gy"), None, None),
            P(("gx", "gy"), None, None),
            P(("gx", "gy"), None, None),
        ),
        out_specs=P(("gx", "gy"), None, None),
        check_vma=False,
    )
```

```python
import jax
import jax.numpy as jnp
from jax import lax
from jax.experimental import pallas as pl
from jax.experimental.pallas import tpu as pltpu
from jax.sharding import PartitionSpec as P

MESH = pl.DeviceIdType.MESH
LANES = 128
VMEM_LIMIT = 46000000
FINISH_LIMIT = 16 * 1024 * 1024


STEPS = 10
CORNER, MIDDLE = 0, 1
FIRST = (0, 3, 5, 7)
FINISH_COLS = 512


def place(role, j, k, h):
    if j == 1:
        return FIRST[k] + 1 - h, 0
    if j == 2:
        return FIRST[k] + h, 1
    if j == 3 and k == 0:
        return 2, h
    if role == CORNER:
        if j == 3 and k == 3:
            return 9, h
        first = {(0, 1): 0, (0, 2): 2, (0, 3): 4, (3, 1): 6, (3, 2): 8}[j, k]
        return first + h, 2
    if j == 0 and k == 1:
        return (8, 2) if h == 0 else (9, 0)
    if j == 3 and k == 1:
        return 9, 1 + h
    first = {(0, 2): 0, (0, 3): 2, (3, 2): 4, (3, 3): 6}[j, k]
    return first + h, 2


def arrival(role, j, k, h):
    if role == MIDDLE and k == 1 and j in (0, 3):
        return h if j == 0 else 4 + h
    return place(role, j, k, h)[0]


def blocks():
    return [(j, k) for j in range(4) for k in range(4) if (j, k) != (0, 0)]


def arrivals(role, step):
    filled = []
    for j, k in blocks():
        for h in range(2):
            (s, link), come = place(role, j, k, h), arrival(role, j, k, h)
            for q in (0, 1) if s == STEPS - 1 else (None,):
                if step == (come + q if come == STEPS - 1 else come):
                    filled.append((s, link, q))
    ids = [(j, k) for j, k in blocks() if min(arrival(role, j, k, h) for h in range(2)) == step]
    return filled, ids


def sends(role, step):
    out = []

    def put(queue, block, halves, there, ids=True):
        if ids:
            out.append((queue, block, None, there))
        out.extend((queue, block, h, there) for h in halves)

    if step < 0:
        put("x", (0, 0), (1, 0), (1, 0))
        put("y", (0, 0), (0, 1), (2, 0))
        put("in", (0, 0), (0, 1), (0, 1) if role == CORNER else (0, 2))
        if role == MIDDLE:
            put("out", (0, 0), (0, 1), (0, 1))
    if step == 0:
        put("x", (2, 0), (0,), (3, 0))
        put("y", (1, 0), (1,), (3, 0), ids=False)
    columns = {1: (1,), 3: (2,), 5: (3,)} if role == CORNER else {1: (1, 2), 3: (3,)}
    for k in columns.get(step, ()):
        put("x", (0, k), (1, 0), (1, k))
        put("y", (0, k), (0, 1), (2, k))
    if role == CORNER:
        if step == 2:
            put("in", (3, 0), (0, 1), (3, 1))
        if step == 7:
            put("x", (2, 3), (0,), (3, 3))
            put("y", (1, 3), (1,), (3, 3), ids=False)
        return out
    if step in (0, 1):
        put("out", (0, 2), (step,), (0, 2), ids=step == 0)
        put("in", (0, 1), (step,), (0, 3), ids=step == 0)
    if step == 2:
        put("out", (0, 3), (0,), (0, 3))
        put("in", (3, 0), (0, 1), (3, 2))
    if step == 3:
        put("out", (0, 3), (1,), (0, 3), ids=False)
        put("out", (3, 0), (0, 1), (3, 1))
    if step in (4, 5):
        put("out", (3, 2), (step - 4,), (3, 2), ids=step == 4)
        put("in", (3, 1), (step - 4,), (3, 3), ids=step == 4)
    return out


def receiver(role, queue):
    if queue in ("x", "y"):
        return role
    return CORNER if queue == "out" else MIDDLE


def packed_tables():
    words = []
    for role in (CORNER, MIDDLE):
        held = {place(role, j, k, h): (j * 4 + k) * 2 + h for j, k in blocks() for h in range(2)}
        words.append([
            [sum(held[s, link] << (5 * (s % 6)) for s in range(first, min(first + 6, STEPS))) for first in (0, 6)]
            for link in range(3)
        ])
    return words


def gather_kernel(
    x_hbm, ids_hbm, wg_hbm, wu_hbm, e_hbm, out_ref, error_ref,
    own, tok, idb, wg, wu, hid, acc, error, turned, mask,
    s_send, s_recv, s_idr, s_pair, s_part, s_load,
):
    gx = lax.axis_index("gx")
    z = lax.axis_index("gy")
    rows, width = x_hbm.shape
    half = rows // 2
    quarter = rows // 4
    lot = 3 * rows
    core = gx % 2
    px = (gx // 2) % 2
    py = gx // 4
    expert = gx * 4 + z
    mirror = z // 2
    inner = z + (3 - 2 * z) * mirror

    def dev(a, b, c):
        return b * 4 + a * 2 + c

    inward = z + 1 - 2 * mirror
    target = {
        "x": (dev(1 - px, py, core), z),
        "y": (dev(px, 1 - py, core), z),
        "in": (gx, inward),
        "out": (gx, z - 1 + 2 * mirror),
        "pair": (dev(px, py, 1 - core), z),
    }

    def remote(src, dst, ssem, rsem, to):
        return pltpu.make_async_remote_copy(
            src_ref=src, dst_ref=dst, send_sem=ssem, recv_sem=rsem,
            device_id=target[to], device_id_type=MESH,
        )

    def spot(s, link, c, q=None):
        if s < STEPS - 1:
            first, count = ((link * 2 + c) * half, half) if q is None else ((link * 2 + c) * half + q * quarter, quarter)
        else:
            first, count = (q * 6 + link * 2 + c) * quarter, quarter
        return tok.at[s, pl.ds(first, count), :]

    def cuts(*steps):
        return (0, 1) if max(steps) == STEPS - 1 else (None,)

    def number(j, k):
        return j * 4 + k

    order = {}
    for role in (CORNER, MIDDLE):
        n = 0
        for step in range(-1, STEPS):
            for item in sends(role, step):
                order[role, item] = n
                n += 2

    def send_copies(role, item):
        queue, (j, k), h, there = item
        far = receiver(role, queue)
        n = order[role, item]
        if h is None:
            src = ids_hbm if (j, k) == (0, 0) else idb.at[number(j, k), core]
            return [remote(src, idb.at[number(*there), core], s_send.at[n], s_idr.at[number(*there)], queue)]
        s, link = place(far, *there, h)
        mine = None if (j, k) == (0, 0) else place(role, j, k, h)
        copies = []
        for q in cuts(s, 0 if mine is None else mine[0]):
            if mine is not None:
                src = spot(*mine, core, q)
            elif q is None:
                src = x_hbm.at[pl.ds(h * half, half), :]
            else:
                src = x_hbm.at[pl.ds(h * half + q * quarter, quarter), :]
            to = s + q if s == STEPS - 1 else s
            copies.append(remote(src, spot(s, link, core, q), s_send.at[n + (q or 0)], s_recv.at[to, link], queue))
        return copies

    def pair_piece(s, link, q):
        n = (s + (q or 0)) * 3 + link
        return remote(spot(s, link, core, q), spot(s, link, core, q), s_pair.at[n], s_part.at[n], "pair")

    def pair_ids(b):
        n = 3 * STEPS + 3 + b
        src = ids_hbm if b == 0 else idb.at[b, core]
        return remote(src, idb.at[b, core], s_pair.at[n], s_part.at[n], "pair")

    n_own = 3 * STEPS + 19
    pair_own = remote(x_hbm, own.at[pl.ds(core * rows, rows), :], s_pair.at[n_own], s_part.at[n_own], "pair")

    def wait_piece(s, link, q):
        here = spot(s, link, core, q)
        remote(here, here, s_send.at[0], s_recv.at[s + (q or 0), link], "pair").wait_recv()

    def wait_ids(b):
        remote(idb.at[b, core], idb.at[b, core], s_send.at[0], s_idr.at[b], "pair").wait_recv()

    def wait_pair_piece(s, link, q):
        n = (s + (q or 0)) * 3 + link
        there = spot(s, link, 1 - core, q)
        remote(there, there, s_send.at[0], s_part.at[n], "pair").wait_recv()

    def wait_pair_ids(b):
        n = 3 * STEPS + 3 + b
        remote(idb.at[b, 1 - core], idb.at[b, 1 - core], s_send.at[0], s_part.at[n], "pair").wait_recv()

    bands = 3
    features = hid.shape[1]
    band = features // bands

    def turn(b, c):
        hits = jnp.sum((idb[b, c] == expert).astype(jnp.float32), axis=0, keepdims=True)
        return jnp.broadcast_to(hits, (LANES, rows)).T

    def hidden(rows_in, count, base):
        live = jnp.concatenate([mask[pl.ds(0, count), :]] * (band // LANES), axis=1)
        for n in range(bands):
            cols = pl.ds(n * band, band)
            gate = jnp.dot(rows_in, wg[:, cols], preferred_element_type=jnp.float32)
            upward = jnp.dot(rows_in, wu[:, cols], preferred_element_type=jnp.float32)
            value = gate / (1.0 + jnp.exp(-gate)) * upward
            hid[pl.ds(base, count), cols] = jnp.where(live > 0.5, value, 0.0).astype(jnp.bfloat16)

    def gram(count, start, base=0):
        for n in range(bands):
            rest = pl.ds(n * band, features - n * band)
            part = lax.dot_general(
                hid[pl.ds(base, count), pl.ds(n * band, band)], hid[pl.ds(base, count), rest],
                (((0,), (0,)), ((), ())), preferred_element_type=jnp.float32,
            )
            if start:
                acc[pl.ds(n * band, band), rest] = part
            else:
                acc[pl.ds(n * band, band), rest] += part

    tables = packed_tables()

    def entry(link, s):
        corner, middle = tables[CORNER][link], tables[MIDDLE][link]
        low = corner[0] + (middle[0] - corner[0]) * inner
        high = corner[1] + (middle[1] - corner[1]) * inner
        word = low + (high - low) * (s // 6)
        return (word >> (5 * (s % 6))) % 32

    def marks(s, size, q=0):
        for link in range(3):
            held = entry(link, s)
            b, h = held // 2, held % 2
            for c in range(2):
                turned[link * 2 + c] = turn(b, c)
                first = pl.multiple_of(h * half + q * size, size)
                mask[pl.ds((link * 2 + c) * size, size), :] = turned[link * 2 + c, pl.ds(first, size), :]

    barrier = pltpu.get_barrier_semaphore()
    for to in ("x", "y", "in", "pair"):
        pl.semaphore_signal(barrier, inc=1, device_id=target[to], device_id_type=MESH)

    @pl.when(inner == 1)
    def _():
        pl.semaphore_signal(barrier, inc=1, device_id=target["out"], device_id_type=MESH)

    local = pltpu.make_async_copy(x_hbm, own.at[pl.ds(core * rows, rows), :], s_load.at[0])
    local_ids = pltpu.make_async_copy(ids_hbm, idb.at[0, core], s_load.at[1])
    load_g = pltpu.make_async_copy(wg_hbm, wg, s_load.at[2])
    load_u = pltpu.make_async_copy(wu_hbm, wu, s_load.at[3])
    load_e = pltpu.make_async_copy(e_hbm, error, s_load.at[4])
    local.start()
    local_ids.start()
    load_g.start()
    load_u.start()
    pl.semaphore_wait(barrier, 4 + inner)

    roles = ((CORNER, inner == 0), (MIDDLE, inner == 1))
    for role, here in roles:
        @pl.when(here)
        def _():
            for item in sends(role, -1):
                [copy.start() for copy in send_copies(role, item)]

    pair_ids(0).start()
    pair_own.start()
    local.wait()
    local_ids.wait()
    wait_pair_ids(0)
    theirs = own.at[pl.ds((1 - core) * rows, rows), :]
    remote(theirs, theirs, s_send.at[0], s_part.at[n_own], "pair").wait_recv()
    load_g.wait()
    load_u.wait()
    load_e.start()
    for c in range(2):
        mask[pl.ds(c * rows, rows), :] = turn(0, c)
    hidden(own[...], 2 * rows, 0)
    gram(2 * rows, True)

    def drain(role, step):
        for item in sends(role, step):
            for copy in send_copies(role, item):
                copy.wait_send()
        if step < 0:
            pair_ids(0).wait_send()
            pair_own.wait_send()
            return
        filled, ids = arrivals(role, step)
        for j, k in ids:
            pair_ids(number(j, k)).wait_send()
        for slot in filled:
            pair_piece(*slot).wait_send()

    def take(role, step):
        filled, ids = arrivals(role, step)
        for j, k in ids:
            wait_ids(number(j, k))
        for slot in filled:
            wait_piece(*slot)
        for item in sends(role, step):
            for copy in send_copies(role, item):
                copy.start()
        for j, k in ids:
            pair_ids(number(j, k)).start()
        for slot in filled:
            pair_piece(*slot).start()

    def join(role, step):
        filled, ids = arrivals(role, step)
        for j, k in ids:
            wait_pair_ids(number(j, k))
        for slot in filled:
            wait_pair_piece(*slot)

    late = 5

    def when_role(act, *args):
        for role, here in roles:
            @pl.when(here)
            def _():
                act(role, *args)

    def at_step(act, s, steps):
        for role, here in roles:
            for step in steps:
                @pl.when(jnp.logical_and(here, s == step))
                def _():
                    act(role, step)

    full = range(STEPS - 1)

    def loop(s, carry):
        at_step(take, s, full)
        at_step(lambda role, step: drain(role, step - late), s, full[late - 1:])

        @pl.when(jnp.logical_and(s > 0, s % 2 == 0))
        def _():
            gram(2 * lot, False)

        @pl.when(s == 1)
        def _():
            load_e.wait()

            def narrow(n, carry):
                some = pl.ds(pl.multiple_of(n * LANES, LANES), LANES)
                error_ref[some, :] = error[some, :].astype(jnp.bfloat16)
                return carry

            lax.fori_loop(0, features // LANES, narrow, 0)

        at_step(join, s, full)
        marks(s, half)
        hidden(tok[s], lot, pl.multiple_of((s % 2) * lot, lot))
        return carry

    lax.fori_loop(0, STEPS - 1, loop, 0)
    last = STEPS - 1
    part = 6 * quarter
    for q in range(2):
        when_role(take, last + q)
        gram(part if q else lot, False, lot if q else 0)
        when_role(drain, last + q - late)
        when_role(join, last + q)
        marks(last, quarter, q)
        hidden(tok[last, pl.ds(q * part, part), :], part, lot if q == 0 else lot + part)
    gram(part, False, lot + part)
    count = jnp.sum((idb[...] == expert).astype(jnp.float32))
    for n in range(bands):
        for m in range(n, bands):
            part = acc[pl.ds(n * band, band), pl.ds(m * band, band)] / count
            out_ref[pl.ds(n * band, band), pl.ds(m * band, band)] = part.astype(out_ref.dtype)
            if m > n:
                out_ref[pl.ds(m * band, band), pl.ds(n * band, band)] = part.T.astype(out_ref.dtype)
    for role, here in roles:
        @pl.when(here)
        def _():
            for step in range(STEPS + 1 - late, STEPS + 1):
                drain(role, step)


def finish_kernel(gram_ref, error_ref, out_hbm, done, sem):
    turns, _, cols = done.shape

    def put(n):
        return pltpu.make_async_copy(done.at[n], out_hbm.at[:, pl.ds(n * cols, cols)], sem.at[n])

    for n in range(turns):
        done[n] = jnp.dot(
            gram_ref[...], error_ref[:, pl.ds(n * cols, cols)],
            preferred_element_type=jnp.float32,
        )
        put(n).start()
    for n in range(turns):
        put(n).wait()


def fused_local(tokens, expert_ids, w_gate, w_up, down_error):
    rows, width = tokens.shape
    top = expert_ids.shape[1]
    features = w_gate.shape[2]
    vmem = pl.BlockSpec(memory_space=pltpu.VMEM)
    hbm = pl.BlockSpec(memory_space=pltpu.HBM)
    dma = pltpu.SemaphoreType.DMA
    n_sends = 2 * max(sum(len(sends(role, step)) for step in range(-1, STEPS)) for role in (CORNER, MIDDLE))
    pieces = 3 * STEPS + 20
    mean_gram, narrow_error = pl.pallas_call(
        gather_kernel,
        out_shape=(
            jax.ShapeDtypeStruct((features, features), jnp.bfloat16),
            jax.ShapeDtypeStruct((features, width), jnp.bfloat16),
        ),
        in_specs=[hbm] * 5,
        out_specs=(vmem, vmem),
        scratch_shapes=[
            pltpu.VMEM((2 * rows, width), jnp.bfloat16),
            pltpu.VMEM((STEPS, 3 * rows, width), jnp.bfloat16),
            pltpu.VMEM((16, 2, top, rows), jnp.int32),
            pltpu.VMEM((width, features), jnp.bfloat16),
            pltpu.VMEM((width, features), jnp.bfloat16),
            pltpu.VMEM((6 * rows, features), jnp.bfloat16),
            pltpu.VMEM((features, features), jnp.float32),
            pltpu.VMEM((features, width), jnp.float32),
            pltpu.VMEM((6, rows, LANES), jnp.float32),
            pltpu.VMEM((3 * rows, LANES), jnp.float32),
            dma((n_sends,)), dma((STEPS + 1, 3)), dma((16,)), dma((pieces,)), dma((pieces,)), dma((5,)),
        ],
        compiler_params=pltpu.CompilerParams(
            collective_id=0, has_side_effects=True, vmem_limit_bytes=VMEM_LIMIT
        ),
    )(*[
        pltpu.with_memory_space_constraint(a, pltpu.HBM)
        for a in (tokens, expert_ids.T, w_gate[0], w_up[0], down_error[0])
    ])
    return pl.pallas_call(
        finish_kernel,
        out_shape=jax.ShapeDtypeStruct(down_error.shape[1:], jnp.float32),
        in_specs=[vmem, vmem],
        out_specs=hbm,
        scratch_shapes=[pltpu.VMEM((down_error.shape[2] // FINISH_COLS, features, FINISH_COLS), jnp.float32), dma((down_error.shape[2] // FINISH_COLS,))],
        compiler_params=pltpu.CompilerParams(vmem_limit_bytes=FINISH_LIMIT),
    )(mean_gram, narrow_error)[None]


def hidden_rows(received, w_gate, w_up):
    sources, slots, width = received.shape
    flat_rows = received.reshape(sources * slots, width)
    gate = jnp.dot(flat_rows, w_gate[0], preferred_element_type=jnp.float32)
    upward = jnp.dot(flat_rows, w_up[0], preferred_element_type=jnp.float32)
    hidden = (jax.nn.silu(gate) * upward).astype(jnp.bfloat16)
    return hidden.reshape(sources, slots, hidden.shape[1])


def cross_gram(first, second):
    return lax.dot_general(
        first, second, (((0,), (0,)), ((), ())), preferred_element_type=jnp.float32
    )


def gram_of(hidden):
    middle = hidden.shape[1] // 2
    left_part = hidden[:, :middle]
    right_part = hidden[:, middle:]
    upper_left = cross_gram(left_part, left_part)
    upper_right = cross_gram(left_part, right_part)
    lower_right = cross_gram(right_part, right_part)
    top_band = jnp.concatenate([upper_left, upper_right], axis=1)
    bottom_band = jnp.concatenate([upper_right.T, lower_right], axis=1)
    return jnp.concatenate([top_band, bottom_band], axis=0)


def local(tokens, expert_ids, w_gate, w_up, down_error):
    across = lax.axis_size("gx")
    within = lax.axis_size("gy")
    experts = across * within
    tok_count, top_count = expert_ids.shape
    width = tokens.shape[1]
    assigned = tok_count * top_count
    capacity = 3 * assigned // experts
    flat_ids = expert_ids.reshape(assigned)
    onehot = (flat_ids[:, None] == jnp.arange(experts, dtype=jnp.int32)[None, :]).astype(
        jnp.bfloat16
    )
    positions = jnp.arange(assigned, dtype=jnp.int32)
    lower = (positions[:, None] >= positions[None, :]).astype(jnp.bfloat16)
    running = jnp.dot(lower, onehot, preferred_element_type=jnp.float32)
    slot_of = (jnp.sum(running * onehot, axis=1) - 1.0).astype(jnp.int32)
    target = flat_ids * capacity + slot_of
    picked = tokens[positions // top_count]
    outgoing = jnp.zeros((experts * capacity, width), jnp.bfloat16).at[target].set(picked)
    tallies = jnp.sum(onehot.astype(jnp.float32), axis=0)
    loads = lax.psum_scatter(tallies, ("gx", "gy"), scatter_dimension=0, tiled=True)
    hidden = hidden_rows(
        lax.all_to_all(
            outgoing.reshape(experts, capacity, width),
            ("gx", "gy"),
            split_axis=0,
            concat_axis=0,
            tiled=True,
        ),
        w_gate,
        w_up,
    )
    hidden = hidden.reshape(experts * capacity, hidden.shape[2])
    gram = gram_of(hidden)
    mean_gram = gram / loads[0]
    product = jnp.dot(
        mean_gram,
        down_error[0],
        preferred_element_type=jnp.float32,
        precision=lax.Precision.HIGHEST,
    )
    return product[None]


def solution(mesh):
    small = mesh.shape["gx"] == 8 and mesh.shape["gy"] == 4
    return jax.shard_map(
        fused_local if small else local,
        mesh=mesh,
        in_specs=(
            P(("gx", "gy"), None),
            P(("gx", "gy"), None),
            P(("gx", "gy"), None, None),
            P(("gx", "gy"), None, None),
            P(("gx", "gy"), None, None),
        ),
        out_specs=P(("gx", "gy"), None, None),
        check_vma=False,
    )
```

```python
import jax
import jax.numpy as jnp
from jax import lax
from jax.experimental import pallas as pl
from jax.experimental.pallas import tpu as pltpu
from jax.sharding import PartitionSpec as P

MESH = pl.DeviceIdType.MESH
LANES = 128
VMEM_LIMIT = 46000000
FINISH_LIMIT = 16 * 1024 * 1024


STEPS = 10
CORNER, MIDDLE = 0, 1
FIRST = (0, 3, 5, 7)
FINISH_COLS = 512


def place(role, j, k, h):
    if j == 1:
        return FIRST[k] + 1 - h, 0
    if j == 2:
        return FIRST[k] + h, 1
    if j == 3 and k == 0:
        return 2, h
    if role == CORNER:
        if j == 3 and k == 3:
            return 9, h
        first = {(0, 1): 0, (0, 2): 2, (0, 3): 4, (3, 1): 6, (3, 2): 8}[j, k]
        return first + h, 2
    if j == 0 and k == 1:
        return (8, 2) if h == 0 else (9, 0)
    if j == 3 and k == 1:
        return 9, 1 + h
    first = {(0, 2): 0, (0, 3): 2, (3, 2): 4, (3, 3): 6}[j, k]
    return first + h, 2


def arrival(role, j, k, h):
    if role == MIDDLE and k == 1 and j in (0, 3):
        return h if j == 0 else 4 + h
    return place(role, j, k, h)[0]


def blocks():
    return [(j, k) for j in range(4) for k in range(4) if (j, k) != (0, 0)]


def ids_arrival(role, j, k):
    return max(0, min(arrival(role, j, k, h) for h in range(2)) - 1)


def arrivals(role, step):
    filled = []
    for j, k in blocks():
        for h in range(2):
            (s, link), come = place(role, j, k, h), arrival(role, j, k, h)
            for q in (0, 1) if s == STEPS - 1 else (None,):
                if step == (come + q if come == STEPS - 1 else come):
                    filled.append((s, link, q))
    ids = [(j, k) for j, k in blocks() if ids_arrival(role, j, k) == step]
    return filled, ids


def sends(role, step):
    out = []

    def put(queue, block, halves, there, ids=True):
        if ids:
            out.append((queue, block, None, there))
        out.extend((queue, block, h, there) for h in halves)

    if step < 0:
        put("x", (0, 0), (1, 0), (1, 0))
        put("y", (0, 0), (0, 1), (2, 0))
        put("in", (0, 0), (0, 1), (0, 1) if role == CORNER else (0, 2))
        if role == MIDDLE:
            put("out", (0, 0), (0, 1), (0, 1))
    if step == 0:
        put("x", (2, 0), (0,), (3, 0))
        put("y", (1, 0), (1,), (3, 0), ids=False)
    columns = {1: (1,), 3: (2,), 5: (3,)} if role == CORNER else {1: (1, 2), 3: (3,)}
    for k in columns.get(step, ()):
        put("x", (0, k), (1, 0), (1, k))
        put("y", (0, k), (0, 1), (2, k))
    if role == CORNER:
        if step == 2:
            put("in", (3, 0), (0, 1), (3, 1))
        if step == 7:
            put("x", (2, 3), (0,), (3, 3))
            put("y", (1, 3), (1,), (3, 3), ids=False)
        return out
    if step in (0, 1):
        put("out", (0, 2), (step,), (0, 2), ids=step == 0)
        put("in", (0, 1), (step,), (0, 3), ids=step == 0)
    if step == 2:
        put("out", (0, 3), (0,), (0, 3))
        put("in", (3, 0), (0, 1), (3, 2))
    if step == 3:
        put("out", (0, 3), (1,), (0, 3), ids=False)
        put("out", (3, 0), (0, 1), (3, 1))
    if step in (4, 5):
        put("out", (3, 2), (step - 4,), (3, 2), ids=step == 4)
        put("in", (3, 1), (step - 4,), (3, 3), ids=step == 4)
    return out


def receiver(role, queue):
    if queue in ("x", "y"):
        return role
    return CORNER if queue == "out" else MIDDLE


def packed_tables():
    words = []
    for role in (CORNER, MIDDLE):
        held = {place(role, j, k, h): (j * 4 + k) * 2 + h for j, k in blocks() for h in range(2)}
        words.append([
            [sum(held[s, link] << (5 * (s % 6)) for s in range(first, min(first + 6, STEPS))) for first in (0, 6)]
            for link in range(3)
        ])
    return words


def gather_kernel(
    x_hbm, ids_hbm, wg_hbm, wu_hbm, e_hbm, out_ref, error_ref,
    own, tok, idb, wg, wu, hid, acc, error, turned, mask,
    s_send, s_recv, s_idr, s_pair, s_part, s_load,
):
    gx = lax.axis_index("gx")
    z = lax.axis_index("gy")
    rows, width = x_hbm.shape
    half = rows // 2
    quarter = rows // 4
    lot = 3 * rows
    core = gx % 2
    px = (gx // 2) % 2
    py = gx // 4
    expert = gx * 4 + z
    mirror = z // 2
    inner = z + (3 - 2 * z) * mirror

    def dev(a, b, c):
        return b * 4 + a * 2 + c

    inward = z + 1 - 2 * mirror
    target = {
        "x": (dev(1 - px, py, core), z),
        "y": (dev(px, 1 - py, core), z),
        "in": (gx, inward),
        "out": (gx, z - 1 + 2 * mirror),
        "pair": (dev(px, py, 1 - core), z),
    }

    def remote(src, dst, ssem, rsem, to):
        return pltpu.make_async_remote_copy(
            src_ref=src, dst_ref=dst, send_sem=ssem, recv_sem=rsem,
            device_id=target[to], device_id_type=MESH,
        )

    def spot(s, link, c, q=None):
        if s < STEPS - 1:
            first, count = ((c * 3 + link) * half, half) if q is None else ((c * 3 + link) * half + q * quarter, quarter)
        else:
            first, count = (q * 6 + c * 3 + link) * quarter, quarter
        return tok.at[s, pl.ds(first, count), :]

    def cuts(*steps):
        return (0, 1) if max(steps) == STEPS - 1 else (None,)

    def number(j, k):
        return j * 4 + k

    order = {}
    for role in (CORNER, MIDDLE):
        n = 0
        for step in range(-1, STEPS):
            for item in sends(role, step):
                order[role, item] = n
                n += 2

    def send_copies(role, item):
        queue, (j, k), h, there = item
        far = receiver(role, queue)
        n = order[role, item]
        if h is None:
            src = idb.at[number(j, k), core]
            return [remote(src, idb.at[number(*there), core], s_send.at[n], s_idr.at[number(*there)], queue)]
        s, link = place(far, *there, h)
        mine = None if (j, k) == (0, 0) else place(role, j, k, h)
        copies = []
        for q in cuts(s, 0 if mine is None else mine[0]):
            if mine is not None:
                src = spot(*mine, core, q)
            elif q is None:
                src = own.at[pl.ds(core * rows + h * half, half), :]
            else:
                src = own.at[pl.ds(core * rows + h * half + q * quarter, quarter), :]
            to = s + q if s == STEPS - 1 else s
            copies.append(remote(src, spot(s, link, core, q), s_send.at[n + (q or 0)], s_recv.at[to, link], queue))
        return copies

    def pair_piece(s, link, q):
        n = (s + (q or 0)) * 3 + link
        return remote(spot(s, link, core, q), spot(s, link, core, q), s_pair.at[n], s_part.at[n], "pair")

    def pair_ids(b):
        n = 3 * STEPS + 3 + b
        return remote(idb.at[b, core], idb.at[b, core], s_pair.at[n], s_part.at[n], "pair")

    n_own = 3 * STEPS + 19
    mine = own.at[pl.ds(core * rows, rows), :]
    pair_own = remote(mine, mine, s_pair.at[n_own], s_part.at[n_own], "pair")

    def wait_piece(s, link, q):
        here = spot(s, link, core, q)
        remote(here, here, s_send.at[0], s_recv.at[s + (q or 0), link], "pair").wait_recv()

    def wait_ids(b):
        remote(idb.at[b, core], idb.at[b, core], s_send.at[0], s_idr.at[b], "pair").wait_recv()

    def wait_pair_piece(s, link, q):
        n = (s + (q or 0)) * 3 + link
        there = spot(s, link, 1 - core, q)
        remote(there, there, s_send.at[0], s_part.at[n], "pair").wait_recv()

    def wait_pair_ids(b):
        n = 3 * STEPS + 3 + b
        remote(idb.at[b, 1 - core], idb.at[b, 1 - core], s_send.at[0], s_part.at[n], "pair").wait_recv()

    bands = 3
    features = hid.shape[1]
    band = features // bands

    def hits(b, c):
        return jnp.sum((idb[b, c] == expert).astype(jnp.float32), axis=0, keepdims=True)

    def turn(rows_of):
        spare = jnp.zeros((8 - len(rows_of), rows), jnp.float32)
        turned[...] = jnp.concatenate(rows_of + [spare], axis=0).T

    def spread(group, first, count, to):
        mask[pl.ds(to, count), :] = jnp.broadcast_to(turned[pl.ds(first, count), group:group + 1], (count, LANES))

    def hidden(rows_in, count, base, first=0, between=None):
        live = jnp.concatenate([mask[pl.ds(first, count), :]] * (band // LANES), axis=1)
        for n in range(bands):
            cols = pl.ds(n * band, band)
            gate = jnp.dot(rows_in, wg[:, cols], preferred_element_type=jnp.float32)
            upward = jnp.dot(rows_in, wu[:, cols], preferred_element_type=jnp.float32)
            value = gate / (1.0 + jnp.exp(-gate)) * upward
            hid[pl.ds(base, count), cols] = jnp.where(live > 0.5, value, 0.0).astype(jnp.bfloat16)
            if between is not None and n == bands - 2:
                between()

    def gram(count, start, base=0):
        for n in range(bands):
            rest = pl.ds(n * band, features - n * band)
            part = lax.dot_general(
                hid[pl.ds(base, count), pl.ds(n * band, band)], hid[pl.ds(base, count), rest],
                (((0,), (0,)), ((), ())), preferred_element_type=jnp.float32,
            )
            if start:
                acc[pl.ds(n * band, band), rest] = part
            else:
                acc[pl.ds(n * band, band), rest] += part

    tables = packed_tables()

    def entry(link, s):
        corner, middle = tables[CORNER][link], tables[MIDDLE][link]
        low = corner[0] + (middle[0] - corner[0]) * inner
        high = corner[1] + (middle[1] - corner[1]) * inner
        word = low + (high - low) * (s // 6)
        return (word >> (5 * (s % 6))) % 32

    def marks(s, size, parts=1, base=0):
        held = [entry(link, s) for link in range(3)]
        turn([hits(held[link] // 2, c) for c in range(2) for link in range(3)])
        for q in range(parts):
            for group in range(6):
                first = pl.multiple_of(held[group % 3] % 2 * half + q * size, size)
                spread(group, first, size, base + (q * 6 + group) * size)

    barrier = pltpu.get_barrier_semaphore()
    for to in ("x", "y", "in", "pair"):
        pl.semaphore_signal(barrier, inc=1, device_id=target[to], device_id_type=MESH)

    @pl.when(inner == 1)
    def _():
        pl.semaphore_signal(barrier, inc=1, device_id=target["out"], device_id_type=MESH)

    local = pltpu.make_async_copy(x_hbm, mine, s_load.at[0])
    local_ids = pltpu.make_async_copy(ids_hbm, idb.at[0, core], s_load.at[1])
    load_g = pltpu.make_async_copy(wg_hbm, wg, s_load.at[2])
    load_u = pltpu.make_async_copy(wu_hbm, wu, s_load.at[3])
    load_e = pltpu.make_async_copy(e_hbm, error, s_load.at[4])
    local.start()
    local_ids.start()
    load_g.start()
    load_u.start()
    local.wait()
    local_ids.wait()
    pl.semaphore_wait(barrier, 4 + inner)

    roles = ((CORNER, inner == 0), (MIDDLE, inner == 1))
    for role, here in roles:
        @pl.when(here)
        def _():
            for item in sends(role, -1):
                [copy.start() for copy in send_copies(role, item)]

    pair_ids(0).start()
    pair_own.start()
    wait_pair_ids(0)
    theirs = own.at[pl.ds((1 - core) * rows, rows), :]
    remote(theirs, theirs, s_send.at[0], s_part.at[n_own], "pair").wait_recv()
    load_g.wait()
    load_u.wait()
    load_e.start()
    turn([hits(0, c) for c in range(2)])
    for c in range(2):
        spread(c, 0, rows, c * rows)
    hidden(own[...], 2 * rows, 0)
    gram(2 * rows, True)

    def drain(role, step):
        for item in sends(role, step):
            for copy in send_copies(role, item):
                copy.wait_send()
        if step < 0:
            pair_ids(0).wait_send()
            pair_own.wait_send()
            return
        filled, ids = arrivals(role, step)
        for j, k in ids:
            pair_ids(number(j, k)).wait_send()
        for slot in filled:
            pair_piece(*slot).wait_send()

    def take(role, step):
        filled, ids = arrivals(role, step)
        early = ids if step == 0 else []
        for j, k in early:
            wait_ids(number(j, k))
        for slot in filled:
            wait_piece(*slot)
        for item in sends(role, step):
            for copy in send_copies(role, item):
                copy.start()
        for j, k in early:
            pair_ids(number(j, k)).start()
        for slot in filled:
            pair_piece(*slot).start()
        for j, k in ids:
            if (j, k) not in early:
                wait_ids(number(j, k))
                pair_ids(number(j, k)).start()

    def join(role, step):
        filled, ids = arrivals(role, step)
        for j, k in ids:
            wait_pair_ids(number(j, k))
        for slot in filled:
            wait_pair_piece(*slot)

    late = 5

    def when_role(act, *args):
        for role, here in roles:
            @pl.when(here)
            def _():
                act(role, *args)

    def at_step(act, s, steps):
        for role, here in roles:
            for step in steps:
                @pl.when(jnp.logical_and(here, s == step))
                def _():
                    act(role, step)

    full = range(STEPS - 2)

    def loop(s, carry):
        at_step(take, s, full)
        at_step(lambda role, step: drain(role, step - late), s, full[late - 1:])

        @pl.when(s > 0)
        def _():
            gram(lot, False, pl.multiple_of((s + 1) % 2 * lot, lot))

        @pl.when(s == 1)
        def _():
            load_e.wait()

            def narrow(n, carry):
                some = pl.ds(pl.multiple_of(n * LANES, LANES), LANES)
                error_ref[some, :] = error[some, :].astype(jnp.bfloat16)
                return carry

            lax.fori_loop(0, features // LANES, narrow, 0)

        at_step(join, s, full)

        @pl.when(s == 0)
        def _():
            marks(0, half)

        hidden(tok[s], lot, pl.multiple_of((s % 2) * lot, lot))
        marks(s + 1, half)
        return carry

    lax.fori_loop(0, STEPS - 2, loop, 0)
    last = STEPS - 1
    part = 6 * quarter
    def side(c, s, q, base, between=None):
        count = lot // 2 if q is None else part // 2
        skip = 0 if q is None else q * part
        rows_at = pl.multiple_of(skip + c * count, count)
        hidden(
            tok[s, pl.ds(rows_at, count), :], count, pl.multiple_of(base + rows_at, count),
            pl.multiple_of(base + rows_at, count), between,
        )

    when_role(take, last - 1)
    side(core, last - 1, None, 0)
    gram(lot, False, lot)
    when_role(join, last - 1)
    marks(last, quarter, 2, lot)
    side(1 - core, last - 1, None, 0, lambda: when_role(take, last))
    side(core, last, 0, lot)
    gram(lot, False)
    when_role(join, last)
    side(1 - core, last, 0, lot, lambda: when_role(take, last + 1))
    side(core, last, 1, lot)
    for step in range(last - 1 - late, last + 1):
        when_role(drain, step)
    when_role(join, last + 1)
    side(1 - core, last, 1, lot)
    gram(lot, False, lot)
    count = jnp.sum((idb[...] == expert).astype(jnp.float32))
    for n in range(bands):
        for m in range(n, bands):
            part = acc[pl.ds(n * band, band), pl.ds(m * band, band)] / count
            out_ref[pl.ds(n * band, band), pl.ds(m * band, band)] = part.astype(out_ref.dtype)
            if m > n:
                out_ref[pl.ds(m * band, band), pl.ds(n * band, band)] = part.T.astype(out_ref.dtype)
    for role, here in roles:
        @pl.when(here)
        def _():
            drain(role, last + 1)


def finish_kernel(gram_ref, error_ref, out_hbm, done, sem):
    turns, _, cols = done.shape

    def put(n):
        return pltpu.make_async_copy(done.at[n], out_hbm.at[:, pl.ds(n * cols, cols)], sem.at[n])

    for n in range(turns):
        done[n] = jnp.dot(
            gram_ref[...], error_ref[:, pl.ds(n * cols, cols)],
            preferred_element_type=jnp.float32,
        )
        put(n).start()
    for n in range(turns):
        put(n).wait()


def fused_local(tokens, expert_ids, w_gate, w_up, down_error):
    rows, width = tokens.shape
    top = expert_ids.shape[1]
    features = w_gate.shape[2]
    vmem = pl.BlockSpec(memory_space=pltpu.VMEM)
    hbm = pl.BlockSpec(memory_space=pltpu.HBM)
    dma = pltpu.SemaphoreType.DMA
    n_sends = 2 * max(sum(len(sends(role, step)) for step in range(-1, STEPS)) for role in (CORNER, MIDDLE))
    pieces = 3 * STEPS + 20
    mean_gram, narrow_error = pl.pallas_call(
        gather_kernel,
        out_shape=(
            jax.ShapeDtypeStruct((features, features), jnp.bfloat16),
            jax.ShapeDtypeStruct((features, width), jnp.bfloat16),
        ),
        in_specs=[hbm] * 5,
        out_specs=(vmem, vmem),
        scratch_shapes=[
            pltpu.VMEM((2 * rows, width), jnp.bfloat16),
            pltpu.VMEM((STEPS, 3 * rows, width), jnp.bfloat16),
            pltpu.VMEM((16, 2, top, rows), jnp.int32),
            pltpu.VMEM((width, features), jnp.bfloat16),
            pltpu.VMEM((width, features), jnp.bfloat16),
            pltpu.VMEM((6 * rows, features), jnp.bfloat16),
            pltpu.VMEM((features, features), jnp.float32),
            pltpu.VMEM((features, width), jnp.float32),
            pltpu.VMEM((rows, 8), jnp.float32),
            pltpu.VMEM((6 * rows, LANES), jnp.float32),
            dma((n_sends,)), dma((STEPS + 1, 3)), dma((16,)), dma((pieces,)), dma((pieces,)), dma((5,)),
        ],
        compiler_params=pltpu.CompilerParams(
            collective_id=0, has_side_effects=True, vmem_limit_bytes=VMEM_LIMIT
        ),
    )(*[
        pltpu.with_memory_space_constraint(a, pltpu.HBM)
        for a in (tokens, expert_ids.T, w_gate[0], w_up[0], down_error[0])
    ])
    return pl.pallas_call(
        finish_kernel,
        out_shape=jax.ShapeDtypeStruct(down_error.shape[1:], jnp.float32),
        in_specs=[vmem, vmem],
        out_specs=hbm,
        scratch_shapes=[pltpu.VMEM((down_error.shape[2] // FINISH_COLS, features, FINISH_COLS), jnp.float32), dma((down_error.shape[2] // FINISH_COLS,))],
        compiler_params=pltpu.CompilerParams(vmem_limit_bytes=FINISH_LIMIT),
    )(mean_gram, narrow_error)[None]


def hidden_rows(received, w_gate, w_up):
    sources, slots, width = received.shape
    flat_rows = received.reshape(sources * slots, width)
    gate = jnp.dot(flat_rows, w_gate[0], preferred_element_type=jnp.float32)
    upward = jnp.dot(flat_rows, w_up[0], preferred_element_type=jnp.float32)
    hidden = (jax.nn.silu(gate) * upward).astype(jnp.bfloat16)
    return hidden.reshape(sources, slots, hidden.shape[1])


def cross_gram(first, second):
    return lax.dot_general(
        first, second, (((0,), (0,)), ((), ())), preferred_element_type=jnp.float32
    )


def gram_of(hidden):
    middle = hidden.shape[1] // 2
    left_part = hidden[:, :middle]
    right_part = hidden[:, middle:]
    upper_left = cross_gram(left_part, left_part)
    upper_right = cross_gram(left_part, right_part)
    lower_right = cross_gram(right_part, right_part)
    top_band = jnp.concatenate([upper_left, upper_right], axis=1)
    bottom_band = jnp.concatenate([upper_right.T, lower_right], axis=1)
    return jnp.concatenate([top_band, bottom_band], axis=0)


def local(tokens, expert_ids, w_gate, w_up, down_error):
    across = lax.axis_size("gx")
    within = lax.axis_size("gy")
    experts = across * within
    tok_count, top_count = expert_ids.shape
    width = tokens.shape[1]
    assigned = tok_count * top_count
    capacity = 3 * assigned // experts
    flat_ids = expert_ids.reshape(assigned)
    onehot = (flat_ids[:, None] == jnp.arange(experts, dtype=jnp.int32)[None, :]).astype(
        jnp.bfloat16
    )
    positions = jnp.arange(assigned, dtype=jnp.int32)
    lower = (positions[:, None] >= positions[None, :]).astype(jnp.bfloat16)
    running = jnp.dot(lower, onehot, preferred_element_type=jnp.float32)
    slot_of = (jnp.sum(running * onehot, axis=1) - 1.0).astype(jnp.int32)
    target = flat_ids * capacity + slot_of
    picked = tokens[positions // top_count]
    outgoing = jnp.zeros((experts * capacity, width), jnp.bfloat16).at[target].set(picked)
    tallies = jnp.sum(onehot.astype(jnp.float32), axis=0)
    loads = lax.psum_scatter(tallies, ("gx", "gy"), scatter_dimension=0, tiled=True)
    hidden = hidden_rows(
        lax.all_to_all(
            outgoing.reshape(experts, capacity, width),
            ("gx", "gy"),
            split_axis=0,
            concat_axis=0,
            tiled=True,
        ),
        w_gate,
        w_up,
    )
    hidden = hidden.reshape(experts * capacity, hidden.shape[2])
    gram = gram_of(hidden)
    mean_gram = gram / loads[0]
    product = jnp.dot(
        mean_gram,
        down_error[0],
        preferred_element_type=jnp.float32,
        precision=lax.Precision.HIGHEST,
    )
    return product[None]


def solution(mesh):
    small = mesh.shape["gx"] == 8 and mesh.shape["gy"] == 4
    return jax.shard_map(
        fused_local if small else local,
        mesh=mesh,
        in_specs=(
            P(("gx", "gy"), None),
            P(("gx", "gy"), None),
            P(("gx", "gy"), None, None),
            P(("gx", "gy"), None, None),
            P(("gx", "gy"), None, None),
        ),
        out_specs=P(("gx", "gy"), None, None),
        check_vma=False,
    )
```

```python
import jax
import jax.numpy as jnp
from jax import lax
from jax.experimental import pallas as pl
from jax.experimental.pallas import tpu as pltpu
from jax.sharding import PartitionSpec as P

MESH = pl.DeviceIdType.MESH
LANES = 128
VMEM_LIMIT = 46000000
FINISH_LIMIT = 16 * 1024 * 1024


STEPS = 10
CORNER, MIDDLE = 0, 1
FIRST = (0, 3, 5, 7)
FINISH_COLS = 512


def place(role, j, k, h):
    if j == 1:
        return FIRST[k] + 1 - h, 0
    if j == 2:
        return FIRST[k] + h, 1
    if j == 3 and k == 0:
        return 2, h
    if role == CORNER:
        if j == 3 and k == 3:
            return 9, h
        first = {(0, 1): 0, (0, 2): 2, (0, 3): 4, (3, 1): 6, (3, 2): 8}[j, k]
        return first + h, 2
    if j == 0 and k == 1:
        return (8, 2) if h == 0 else (9, 0)
    if j == 3 and k == 1:
        return 9, 1 + h
    first = {(0, 2): 0, (0, 3): 2, (3, 2): 4, (3, 3): 6}[j, k]
    return first + h, 2


def arrival(role, j, k, h):
    if role == MIDDLE and k == 1 and j in (0, 3):
        return h if j == 0 else 4 + h
    return place(role, j, k, h)[0]


def blocks():
    return [(j, k) for j in range(4) for k in range(4) if (j, k) != (0, 0)]


def ids_arrival(role, j, k):
    return max(0, min(arrival(role, j, k, h) for h in range(2)) - 1)


def arrivals(role, step):
    filled = []
    for j, k in blocks():
        for h in range(2):
            (s, link), come = place(role, j, k, h), arrival(role, j, k, h)
            for q in (0, 1) if s == STEPS - 1 else (None,):
                if step == (come + q if come == STEPS - 1 else come):
                    filled.append((s, link, q))
    ids = [(j, k) for j, k in blocks() if ids_arrival(role, j, k) == step]
    return filled, ids


def sends(role, step):
    out = []

    def put(queue, block, halves, there, ids=True):
        if ids:
            out.append((queue, block, None, there))
        out.extend((queue, block, h, there) for h in halves)

    if step < 0:
        put("x", (0, 0), (1, 0), (1, 0))
        put("y", (0, 0), (0, 1), (2, 0))
        put("in", (0, 0), (0, 1), (0, 1) if role == CORNER else (0, 2))
        if role == MIDDLE:
            put("out", (0, 0), (0, 1), (0, 1))
    if step == 0:
        put("x", (2, 0), (0,), (3, 0))
        put("y", (1, 0), (1,), (3, 0), ids=False)
    columns = {1: (1,), 3: (2,), 5: (3,)} if role == CORNER else {1: (1, 2), 3: (3,)}
    for k in columns.get(step, ()):
        put("x", (0, k), (1, 0), (1, k))
        put("y", (0, k), (0, 1), (2, k))
    if role == CORNER:
        if step == 2:
            put("in", (3, 0), (0, 1), (3, 1))
        if step == 7:
            put("x", (2, 3), (0,), (3, 3))
            put("y", (1, 3), (1,), (3, 3), ids=False)
        return out
    if step in (0, 1):
        put("out", (0, 2), (step,), (0, 2), ids=step == 0)
        put("in", (0, 1), (step,), (0, 3), ids=step == 0)
    if step == 2:
        put("out", (0, 3), (0,), (0, 3))
        put("in", (3, 0), (0, 1), (3, 2))
    if step == 3:
        put("out", (0, 3), (1,), (0, 3), ids=False)
        put("out", (3, 0), (0, 1), (3, 1))
    if step in (4, 5):
        put("out", (3, 2), (step - 4,), (3, 2), ids=step == 4)
        put("in", (3, 1), (step - 4,), (3, 3), ids=step == 4)
    return out


def receiver(role, queue):
    if queue in ("x", "y"):
        return role
    return CORNER if queue == "out" else MIDDLE


def packed_tables():
    words = []
    for role in (CORNER, MIDDLE):
        held = {place(role, j, k, h): (j * 4 + k) * 2 + h for j, k in blocks() for h in range(2)}
        words.append([
            [sum(held[s, link] << (5 * (s % 6)) for s in range(first, min(first + 6, STEPS))) for first in (0, 6)]
            for link in range(3)
        ])
    return words


def gather_kernel(
    x_hbm, ids_hbm, wg_hbm, wu_hbm, e_hbm, out_ref, error_ref,
    own, tok, idb, wg, wu, hid, acc, error, turned, mask,
    s_send, s_recv, s_idr, s_part, s_partid, s_load,
):
    gx = lax.axis_index("gx")
    z = lax.axis_index("gy")
    rows, width = x_hbm.shape
    half = rows // 2
    quarter = rows // 4
    lot = 3 * rows
    core = gx % 2
    px = (gx // 2) % 2
    py = gx // 4
    expert = gx * 4 + z
    mirror = z // 2
    inner = z + (3 - 2 * z) * mirror

    def dev(a, b, c):
        return b * 4 + a * 2 + c

    inward = z + 1 - 2 * mirror
    target = {
        "x": (dev(1 - px, py, core), z),
        "y": (dev(px, 1 - py, core), z),
        "in": (gx, inward),
        "out": (gx, z - 1 + 2 * mirror),
        "pair": (dev(px, py, 1 - core), z),
    }

    def remote(src, dst, ssem, rsem, to):
        return pltpu.make_async_remote_copy(
            src_ref=src, dst_ref=dst, send_sem=ssem, recv_sem=rsem,
            device_id=target[to], device_id_type=MESH,
        )

    def spot(s, link, c, q=None):
        if s < STEPS - 1:
            first, count = ((c * 3 + link) * half, half) if q is None else ((c * 3 + link) * half + q * quarter, quarter)
        else:
            first, count = (q * 6 + c * 3 + link) * quarter, quarter
        return tok.at[s, pl.ds(first, count), :]

    def cuts(*steps):
        return (0, 1) if max(steps) == STEPS - 1 else (None,)

    def number(j, k):
        return j * 4 + k

    def send_copies(role, item):
        queue, (j, k), h, there = item
        far = receiver(role, queue)
        if h is None:
            src, dst = idb.at[number(j, k), core], idb.at[number(*there), core]
            return [remote(src, dst, s_send.at[1], s_idr.at[ids_arrival(far, *there)], queue)]
        s, link = place(far, *there, h)
        come = arrival(far, *there, h)
        mine = None if (j, k) == (0, 0) else place(role, j, k, h)
        copies = []
        for q in cuts(s, 0 if mine is None else mine[0]):
            if mine is not None:
                src = spot(*mine, core, q)
            elif q is None:
                src = own.at[pl.ds(core * rows + h * half, half), :]
            else:
                src = own.at[pl.ds(core * rows + h * half + q * quarter, quarter), :]
            step = come + (q if come == STEPS - 1 else 0)
            copies.append(remote(src, spot(s, link, core, q), s_send.at[0], s_recv.at[step], queue))
        return copies

    def pair_piece(step, slot):
        return remote(spot(*slot[:2], core, slot[2]), spot(*slot[:2], core, slot[2]), s_send.at[2], s_part.at[step], "pair")

    def pair_ids(step, b):
        return remote(idb.at[b, core], idb.at[b, core], s_send.at[3], s_partid.at[step], "pair")

    mine = own.at[pl.ds(core * rows, rows), :]
    pair_own = remote(mine, mine, s_send.at[4], s_part.at[STEPS + 1], "pair")

    def size_of(filled):
        return sum(half if q is None else quarter for _, _, q in filled)

    def counted(count):
        views = [tok.at[pl.ds(0, count // lot)]] if count >= lot else []
        return views + ([tok.at[0, pl.ds(0, count % lot), :]] if count % lot else [])

    def wait_rows(sem, count):
        for view in counted(count):
            remote(view, view, s_send.at[0], sem, "pair").wait_recv()

    def wait_ids(sem, count):
        if count:
            view = idb.at[pl.ds(0, count), 0]
            remote(view, view, s_send.at[0], sem, "pair").wait_recv()

    bands = 3
    features = hid.shape[1]
    band = features // bands

    def hits(b, c):
        return jnp.sum((idb[b, c] == expert).astype(jnp.float32), axis=0, keepdims=True)

    def turn(rows_of):
        spare = jnp.zeros((8 - len(rows_of), rows), jnp.float32)
        turned[...] = jnp.concatenate(rows_of + [spare], axis=0).T

    def spread(group, first, count, to):
        mask[pl.ds(to, count), :] = jnp.broadcast_to(turned[pl.ds(first, count), group:group + 1], (count, LANES))

    def hidden(rows_in, count, base, first=0, between=None, after=1):
        live = jnp.concatenate([mask[pl.ds(first, count), :]] * (band // LANES), axis=1)
        for n in range(bands):
            cols = pl.ds(n * band, band)
            gate = jnp.dot(rows_in, wg[:, cols], preferred_element_type=jnp.float32)
            upward = jnp.dot(rows_in, wu[:, cols], preferred_element_type=jnp.float32)
            value = gate / (1.0 + jnp.exp(-gate)) * upward
            hid[pl.ds(base, count), cols] = jnp.where(live > 0.5, value, 0.0).astype(jnp.bfloat16)
            if between is not None and n == after:
                between()

    def gram(count, start, base=0):
        for n in range(bands):
            rest = pl.ds(n * band, features - n * band)
            part = lax.dot_general(
                hid[pl.ds(base, count), pl.ds(n * band, band)], hid[pl.ds(base, count), rest],
                (((0,), (0,)), ((), ())), preferred_element_type=jnp.float32,
            )
            if start:
                acc[pl.ds(n * band, band), rest] = part
            else:
                acc[pl.ds(n * band, band), rest] += part

    tables = packed_tables()

    def entry(link, s):
        corner, middle = tables[CORNER][link], tables[MIDDLE][link]
        low = corner[0] + (middle[0] - corner[0]) * inner
        high = corner[1] + (middle[1] - corner[1]) * inner
        word = low + (high - low) * (s // 6)
        return (word >> (5 * (s % 6))) % 32

    def marks(s, size, parts=1, base=0):
        held = [entry(link, s) for link in range(3)]
        turn([hits(held[link] // 2, c) for c in range(2) for link in range(3)])
        for q in range(parts):
            for group in range(6):
                first = pl.multiple_of(held[group % 3] % 2 * half + q * size, size)
                spread(group, first, size, base + (q * 6 + group) * size)

    barrier = pltpu.get_barrier_semaphore()
    for to in ("x", "y", "in", "pair"):
        pl.semaphore_signal(barrier, inc=1, device_id=target[to], device_id_type=MESH)

    @pl.when(inner == 1)
    def _():
        pl.semaphore_signal(barrier, inc=1, device_id=target["out"], device_id_type=MESH)

    local = pltpu.make_async_copy(x_hbm, mine, s_load.at[0])
    local_ids = pltpu.make_async_copy(ids_hbm, idb.at[0, core], s_load.at[1])
    load_g = pltpu.make_async_copy(wg_hbm, wg, s_load.at[2])
    load_u = pltpu.make_async_copy(wu_hbm, wu, s_load.at[3])
    load_e = pltpu.make_async_copy(e_hbm, error, s_load.at[4])
    local.start()
    local_ids.start()
    local.wait()
    local_ids.wait()
    pl.semaphore_wait(barrier, 4 + inner)

    roles = ((CORNER, inner == 0), (MIDDLE, inner == 1))
    for role, here in roles:
        @pl.when(here)
        def _():
            for item in sends(role, -1):
                [copy.start() for copy in send_copies(role, item)]

    pair_ids(STEPS + 1, 0).start()
    pair_own.start()
    load_g.start()
    load_u.start()
    wait_ids(s_partid.at[STEPS + 1], 1)
    theirs = own.at[pl.ds((1 - core) * rows, rows), :]
    remote(theirs, theirs, s_send.at[4], s_part.at[STEPS + 1], "pair").wait_recv()
    load_g.wait()
    load_u.wait()
    load_e.start()
    turn([hits(0, c) for c in range(2)])
    for c in range(2):
        spread(c, 0, rows, c * rows)
    hidden(own[...], 2 * rows, 0)
    gram(2 * rows, True)

    def drain(role):
        items = [item for step in range(-1, STEPS) for item in sends(role, step)]
        count = sum(half for item in items if item[2] is not None)
        pairs = sum(size_of(arrivals(role, step)[0]) for step in range(STEPS + 1))
        for n, total in ((0, count), (2, pairs)):
            for view in counted(total):
                remote(view, view, s_send.at[n], s_part.at[0], "pair").wait_send()
        for n, total in ((1, sum(item[2] is None for item in items)), (3, 16)):
            whole, rest = total // 2, total % 2
            for view in [idb.at[pl.ds(0, whole)]] + [idb.at[0, 0]] * rest:
                remote(view, view, s_send.at[n], s_part.at[0], "pair").wait_send()
        pair_own.wait_send()

    def take(role, step):
        filled, ids = arrivals(role, step)
        if step == 0:
            wait_ids(s_idr.at[step], len(ids))
        wait_rows(s_recv.at[step], size_of(filled))
        for item in sends(role, step):
            for copy in send_copies(role, item):
                copy.start()
        if step == 0:
            for j, k in ids:
                pair_ids(step, number(j, k)).start()
        for slot in filled:
            pair_piece(step, slot).start()
        if step and ids:
            wait_ids(s_idr.at[step], len(ids))
            for j, k in ids:
                pair_ids(step, number(j, k)).start()

    def join(role, step):
        filled, ids = arrivals(role, step)
        wait_ids(s_partid.at[step], len(ids))
        wait_rows(s_part.at[step], size_of(filled))

    def when_role(act, *args):
        for role, here in roles:
            @pl.when(here)
            def _():
                act(role, *args)

    def at_step(act, s, steps):
        for role, here in roles:
            for step in steps:
                @pl.when(jnp.logical_and(here, s == step))
                def _():
                    act(role, step)

    full = range(STEPS - 2)

    def loop(s, carry):
        at_step(take, s, full)

        @pl.when(s > 0)
        def _():
            gram(lot, False, pl.multiple_of((s + 1) % 2 * lot, lot))

        @pl.when(s == 1)
        def _():
            load_e.wait()

            def narrow(n, carry):
                some = pl.ds(pl.multiple_of(n * LANES, LANES), LANES)
                error_ref[some, :] = error[some, :].astype(jnp.bfloat16)
                return carry

            lax.fori_loop(0, features // LANES, narrow, 0)

        at_step(join, s, full)

        @pl.when(s == 0)
        def _():
            marks(0, half)

        hidden(tok[s], lot, pl.multiple_of((s % 2) * lot, lot))
        marks(s + 1, half)
        return carry

    lax.fori_loop(0, STEPS - 2, loop, 0)
    last = STEPS - 1
    part = 6 * quarter
    def side(c, s, q, base, between=None, after=1):
        count = lot // 2 if q is None else part // 2
        skip = 0 if q is None else q * part
        rows_at = pl.multiple_of(skip + c * count, count)
        hidden(
            tok[s, pl.ds(rows_at, count), :], count, pl.multiple_of(base + rows_at, count),
            pl.multiple_of(base + rows_at, count), between, after,
        )

    when_role(take, last - 1)
    side(core, last - 1, None, 0)
    gram(lot, False, lot)
    when_role(join, last - 1)
    marks(last, quarter, 2, lot)
    side(1 - core, last - 1, None, 0, lambda: when_role(take, last), 0)
    gram(lot, False)
    when_role(join, last)
    hidden(tok[last, pl.ds(0, part), :], part, lot, lot, lambda: when_role(take, last + 1), 1)
    side(core, last, 1, lot)
    when_role(join, last + 1)
    side(1 - core, last, 1, lot)
    gram(lot, False, lot)
    count = jnp.sum((idb[...] == expert).astype(jnp.float32))
    for n in range(bands):
        for m in range(n, bands):
            part = acc[pl.ds(n * band, band), pl.ds(m * band, band)] / count
            out_ref[pl.ds(n * band, band), pl.ds(m * band, band)] = part.astype(out_ref.dtype)
            if m > n:
                out_ref[pl.ds(m * band, band), pl.ds(n * band, band)] = part.T.astype(out_ref.dtype)
    when_role(drain)


def finish_kernel(gram_ref, error_ref, out_hbm, done, sem):
    turns, features, cols = done.shape

    def put(n, first, count, at):
        return pltpu.make_async_copy(
            done.at[n, pl.ds(first, count), :], out_hbm.at[pl.ds(first, count), pl.ds(n * cols, cols)], sem.at[at]
        )

    blocks = [(n, 0, features) for n in range(turns - 1)]
    blocks += [(turns - 1, first, features // 2) for first in (0, features // 2)]
    for at, (n, first, count) in enumerate(blocks):
        done[n, pl.ds(first, count), :] = jnp.dot(
            gram_ref[pl.ds(first, count), :], error_ref[:, pl.ds(n * cols, cols)],
            preferred_element_type=jnp.float32,
        )
        put(n, first, count, at).start()
    for at, block in enumerate(blocks):
        put(*block, at).wait()


def fused_local(tokens, expert_ids, w_gate, w_up, down_error):
    rows, width = tokens.shape
    top = expert_ids.shape[1]
    features = w_gate.shape[2]
    vmem = pl.BlockSpec(memory_space=pltpu.VMEM)
    hbm = pl.BlockSpec(memory_space=pltpu.HBM)
    dma = pltpu.SemaphoreType.DMA
    mean_gram, narrow_error = pl.pallas_call(
        gather_kernel,
        out_shape=(
            jax.ShapeDtypeStruct((features, features), jnp.bfloat16),
            jax.ShapeDtypeStruct((features, width), jnp.bfloat16),
        ),
        in_specs=[hbm] * 5,
        out_specs=(vmem, vmem),
        scratch_shapes=[
            pltpu.VMEM((2 * rows, width), jnp.bfloat16),
            pltpu.VMEM((STEPS, 3 * rows, width), jnp.bfloat16),
            pltpu.VMEM((16, 2, top, rows), jnp.int32),
            pltpu.VMEM((width, features), jnp.bfloat16),
            pltpu.VMEM((width, features), jnp.bfloat16),
            pltpu.VMEM((6 * rows, features), jnp.bfloat16),
            pltpu.VMEM((features, features), jnp.float32),
            pltpu.VMEM((features, width), jnp.float32),
            pltpu.VMEM((rows, 8), jnp.float32),
            pltpu.VMEM((6 * rows, LANES), jnp.float32),
            dma((5,)), dma((STEPS + 1,)), dma((STEPS,)), dma((STEPS + 2,)), dma((STEPS + 2,)), dma((5,)),
        ],
        compiler_params=pltpu.CompilerParams(
            collective_id=0, has_side_effects=True, vmem_limit_bytes=VMEM_LIMIT
        ),
    )(*[
        pltpu.with_memory_space_constraint(a, pltpu.HBM)
        for a in (tokens, expert_ids.T, w_gate[0], w_up[0], down_error[0])
    ])
    return pl.pallas_call(
        finish_kernel,
        out_shape=jax.ShapeDtypeStruct(down_error.shape[1:], jnp.float32),
        in_specs=[vmem, vmem],
        out_specs=hbm,
        scratch_shapes=[pltpu.VMEM((down_error.shape[2] // FINISH_COLS, features, FINISH_COLS), jnp.float32), dma((down_error.shape[2] // FINISH_COLS + 1,))],
        compiler_params=pltpu.CompilerParams(vmem_limit_bytes=FINISH_LIMIT),
    )(mean_gram, narrow_error)[None]


def hidden_rows(received, w_gate, w_up):
    sources, slots, width = received.shape
    flat_rows = received.reshape(sources * slots, width)
    gate = jnp.dot(flat_rows, w_gate[0], preferred_element_type=jnp.float32)
    upward = jnp.dot(flat_rows, w_up[0], preferred_element_type=jnp.float32)
    hidden = (jax.nn.silu(gate) * upward).astype(jnp.bfloat16)
    return hidden.reshape(sources, slots, hidden.shape[1])


def cross_gram(first, second):
    return lax.dot_general(
        first, second, (((0,), (0,)), ((), ())), preferred_element_type=jnp.float32
    )


def gram_of(hidden):
    middle = hidden.shape[1] // 2
    left_part = hidden[:, :middle]
    right_part = hidden[:, middle:]
    upper_left = cross_gram(left_part, left_part)
    upper_right = cross_gram(left_part, right_part)
    lower_right = cross_gram(right_part, right_part)
    top_band = jnp.concatenate([upper_left, upper_right], axis=1)
    bottom_band = jnp.concatenate([upper_right.T, lower_right], axis=1)
    return jnp.concatenate([top_band, bottom_band], axis=0)


def local(tokens, expert_ids, w_gate, w_up, down_error):
    across = lax.axis_size("gx")
    within = lax.axis_size("gy")
    experts = across * within
    tok_count, top_count = expert_ids.shape
    width = tokens.shape[1]
    assigned = tok_count * top_count
    capacity = 3 * assigned // experts
    flat_ids = expert_ids.reshape(assigned)
    onehot = (flat_ids[:, None] == jnp.arange(experts, dtype=jnp.int32)[None, :]).astype(
        jnp.bfloat16
    )
    positions = jnp.arange(assigned, dtype=jnp.int32)
    lower = (positions[:, None] >= positions[None, :]).astype(jnp.bfloat16)
    running = jnp.dot(lower, onehot, preferred_element_type=jnp.float32)
    slot_of = (jnp.sum(running * onehot, axis=1) - 1.0).astype(jnp.int32)
    target = flat_ids * capacity + slot_of
    picked = tokens[positions // top_count]
    outgoing = jnp.zeros((experts * capacity, width), jnp.bfloat16).at[target].set(picked)
    tallies = jnp.sum(onehot.astype(jnp.float32), axis=0)
    loads = lax.psum_scatter(tallies, ("gx", "gy"), scatter_dimension=0, tiled=True)
    hidden = hidden_rows(
        lax.all_to_all(
            outgoing.reshape(experts, capacity, width),
            ("gx", "gy"),
            split_axis=0,
            concat_axis=0,
            tiled=True,
        ),
        w_gate,
        w_up,
    )
    hidden = hidden.reshape(experts * capacity, hidden.shape[2])
    gram = gram_of(hidden)
    mean_gram = gram / loads[0]
    product = jnp.dot(
        mean_gram,
        down_error[0],
        preferred_element_type=jnp.float32,
        precision=lax.Precision.HIGHEST,
    )
    return product[None]


def solution(mesh):
    small = mesh.shape["gx"] == 8 and mesh.shape["gy"] == 4
    return jax.shard_map(
        fused_local if small else local,
        mesh=mesh,
        in_specs=(
            P(("gx", "gy"), None),
            P(("gx", "gy"), None),
            P(("gx", "gy"), None, None),
            P(("gx", "gy"), None, None),
            P(("gx", "gy"), None, None),
        ),
        out_specs=P(("gx", "gy"), None, None),
        check_vma=False,
    )
```

```python
import jax
import jax.numpy as jnp
from jax import lax
from jax.experimental import pallas as pl
from jax.experimental.pallas import tpu as pltpu
from jax.sharding import PartitionSpec as P

MESH = pl.DeviceIdType.MESH
LANES = 128
VMEM_LIMIT = 46000000
FINISH_LIMIT = 16 * 1024 * 1024


STEPS = 10
CORNER, MIDDLE = 0, 1
FIRST = (0, 3, 5, 7)
FINISH_COLS = 512


def place(role, j, k, h):
    if j == 1:
        return FIRST[k] + 1 - h, 0
    if j == 2:
        return FIRST[k] + h, 1
    if j == 3 and k == 0:
        return 2, h
    if role == CORNER:
        if j == 3 and k == 3:
            return 9, h
        first = {(0, 1): 0, (0, 2): 2, (0, 3): 4, (3, 1): 6, (3, 2): 8}[j, k]
        return first + h, 2
    if j == 0 and k == 1:
        return (8, 2) if h == 0 else (9, 0)
    if j == 3 and k == 1:
        return 9, 1 + h
    first = {(0, 2): 0, (0, 3): 2, (3, 2): 4, (3, 3): 6}[j, k]
    return first + h, 2


def arrival(role, j, k, h):
    if role == MIDDLE and k == 1 and j in (0, 3):
        return h if j == 0 else 4 + h
    return place(role, j, k, h)[0]


def blocks():
    return [(j, k) for j in range(4) for k in range(4) if (j, k) != (0, 0)]


def ids_arrival(role, j, k):
    return max(0, min(arrival(role, j, k, h) for h in range(2)) - 1)


def arrivals(role, step):
    filled = []
    for j, k in blocks():
        for h in range(2):
            (s, link), come = place(role, j, k, h), arrival(role, j, k, h)
            for q in (0, 1) if s == STEPS - 1 else (None,):
                if step == (come + q if come == STEPS - 1 else come):
                    filled.append((s, link, q))
    ids = [(j, k) for j, k in blocks() if ids_arrival(role, j, k) == step]
    return filled, ids


def sends(role, step):
    out = []

    def put(queue, block, halves, there, ids=True):
        if ids:
            out.append((queue, block, None, there))
        out.extend((queue, block, h, there) for h in halves)

    if step < 0:
        put("x", (0, 0), (1, 0), (1, 0))
        put("y", (0, 0), (0, 1), (2, 0))
        put("in", (0, 0), (0, 1), (0, 1) if role == CORNER else (0, 2))
        if role == MIDDLE:
            put("out", (0, 0), (0, 1), (0, 1))
    if step == 0:
        put("x", (2, 0), (0,), (3, 0))
        put("y", (1, 0), (1,), (3, 0), ids=False)
    columns = {1: (1,), 3: (2,), 5: (3,)} if role == CORNER else {1: (1, 2), 3: (3,)}
    for k in columns.get(step, ()):
        put("x", (0, k), (1, 0), (1, k))
        put("y", (0, k), (0, 1), (2, k))
    if role == CORNER:
        if step == 2:
            put("in", (3, 0), (0, 1), (3, 1))
        if step == 7:
            put("x", (2, 3), (0,), (3, 3), ids=False)
            put("y", (1, 3), (1,), (3, 3))
        return out
    if step in (0, 1):
        put("out", (0, 2), (step,), (0, 2), ids=step == 0)
        put("in", (0, 1), (step,), (0, 3), ids=step == 0)
    if step == 2:
        put("out", (0, 3), (0,), (0, 3))
        put("in", (3, 0), (0, 1), (3, 2))
    if step == 3:
        put("out", (0, 3), (1,), (0, 3), ids=False)
        put("out", (3, 0), (0, 1), (3, 1))
    if step in (4, 5):
        put("out", (3, 2), (step - 4,), (3, 2), ids=step == 4)
        put("in", (3, 1), (step - 4,), (3, 3), ids=step == 4)
    return out


def receiver(role, queue):
    if queue in ("x", "y"):
        return role
    return CORNER if queue == "out" else MIDDLE


def packed_tables():
    words = []
    for role in (CORNER, MIDDLE):
        held = {place(role, j, k, h): (j * 4 + k) * 2 + h for j, k in blocks() for h in range(2)}
        words.append([
            [sum(held[s, link] << (5 * (s % 6)) for s in range(first, min(first + 6, STEPS))) for first in (0, 6)]
            for link in range(3)
        ])
    return words


def gather_kernel(
    x_hbm, ids_hbm, wg_hbm, wu_hbm, e_hbm, out_ref, error_ref,
    own, tok, idb, wg, wu, hid, acc, error, turned, mask,
    s_send, s_recv, s_idr, s_part, s_partid, s_load,
):
    gx = lax.axis_index("gx")
    z = lax.axis_index("gy")
    rows, width = x_hbm.shape
    half = rows // 2
    quarter = rows // 4
    lot = 3 * rows
    core = gx % 2
    px = (gx // 2) % 2
    py = gx // 4
    expert = gx * 4 + z
    mirror = z // 2
    inner = z + (3 - 2 * z) * mirror

    def dev(a, b, c):
        return b * 4 + a * 2 + c

    inward = z + 1 - 2 * mirror
    target = {
        "x": (dev(1 - px, py, core), z),
        "y": (dev(px, 1 - py, core), z),
        "in": (gx, inward),
        "out": (gx, z - 1 + 2 * mirror),
        "pair": (dev(px, py, 1 - core), z),
    }

    def remote(src, dst, ssem, rsem, to):
        return pltpu.make_async_remote_copy(
            src_ref=src, dst_ref=dst, send_sem=ssem, recv_sem=rsem,
            device_id=target[to], device_id_type=MESH,
        )

    def spot(s, link, c, q=None):
        if s < STEPS - 1:
            first, count = ((c * 3 + link) * half, half) if q is None else ((c * 3 + link) * half + q * quarter, quarter)
        else:
            first, count = (q * 6 + c * 3 + link) * quarter, quarter
        return tok.at[s, pl.ds(first, count), :]

    def cuts(*steps):
        return (0, 1) if max(steps) == STEPS - 1 else (None,)

    def number(j, k):
        return j * 4 + k

    def send_copies(role, item):
        queue, (j, k), h, there = item
        far = receiver(role, queue)
        if h is None:
            src, dst = idb.at[number(j, k), core], idb.at[number(*there), core]
            return [remote(src, dst, s_send.at[1], s_idr.at[ids_arrival(far, *there)], queue)]
        s, link = place(far, *there, h)
        come = arrival(far, *there, h)
        mine = None if (j, k) == (0, 0) else place(role, j, k, h)
        copies = []
        for q in cuts(s, 0 if mine is None else mine[0]):
            if mine is not None:
                src = spot(*mine, core, q)
            elif q is None:
                src = own.at[pl.ds(core * rows + h * half, half), :]
            else:
                src = own.at[pl.ds(core * rows + h * half + q * quarter, quarter), :]
            step = come + (q if come == STEPS - 1 else 0)
            copies.append(remote(src, spot(s, link, core, q), s_send.at[0], s_recv.at[step], queue))
        return copies

    def pair_piece(step, slot):
        return remote(spot(*slot[:2], core, slot[2]), spot(*slot[:2], core, slot[2]), s_send.at[2], s_part.at[step % 2], "pair")

    def pair_ids(step, b):
        return remote(idb.at[b, core], idb.at[b, core], s_send.at[3], s_partid.at[step % 2], "pair")

    mine = own.at[pl.ds(core * rows, rows), :]
    pair_own = remote(mine, mine, s_send.at[4], s_part.at[1], "pair")

    def size_of(filled):
        return sum(half if q is None else quarter for _, _, q in filled)

    def counted(count):
        views = [tok.at[pl.ds(0, count // lot)]] if count >= lot else []
        return views + ([tok.at[0, pl.ds(0, count % lot), :]] if count % lot else [])

    def wait_rows(sem, count):
        for view in counted(count):
            remote(view, view, s_send.at[0], sem, "pair").wait_recv()

    def wait_ids(sem, count):
        if count:
            view = idb.at[pl.ds(0, count), 0]
            remote(view, view, s_send.at[0], sem, "pair").wait_recv()

    bands = 3
    features = hid.shape[1]
    band = features // bands

    def hits(b, c):
        return jnp.sum((idb[b, c] == expert).astype(jnp.float32), axis=0, keepdims=True)

    def turn(rows_of):
        spare = jnp.zeros((8 - len(rows_of), rows), jnp.float32)
        turned[...] = jnp.concatenate(rows_of + [spare], axis=0).T

    def spread(group, first, count, to):
        mask[pl.ds(to, count), :] = jnp.broadcast_to(turned[pl.ds(first, count), group:group + 1], (count, LANES))

    def hidden(rows_in, count, base, first=0, between=None, after=1):
        live = jnp.concatenate([mask[pl.ds(first, count), :]] * (band // LANES), axis=1)
        for n in range(bands):
            cols = pl.ds(n * band, band)
            gate = jnp.dot(rows_in, wg[:, cols], preferred_element_type=jnp.float32)
            upward = jnp.dot(rows_in, wu[:, cols], preferred_element_type=jnp.float32)
            value = gate / (1.0 + jnp.exp(-gate)) * upward
            hid[pl.ds(base, count), cols] = jnp.where(live > 0.5, value, 0.0).astype(jnp.bfloat16)
            if between is not None and n == after:
                between()

    def gram(count, start, base=0):
        for n in range(bands):
            rest = pl.ds(n * band, features - n * band)
            part = lax.dot_general(
                hid[pl.ds(base, count), pl.ds(n * band, band)], hid[pl.ds(base, count), rest],
                (((0,), (0,)), ((), ())), preferred_element_type=jnp.float32,
            )
            if start:
                acc[pl.ds(n * band, band), rest] = part
            else:
                acc[pl.ds(n * band, band), rest] += part

    tables = packed_tables()

    def entry(link, s):
        corner, middle = tables[CORNER][link], tables[MIDDLE][link]
        low = corner[0] + (middle[0] - corner[0]) * inner
        high = corner[1] + (middle[1] - corner[1]) * inner
        word = low + (high - low) * (s // 6)
        return (word >> (5 * (s % 6))) % 32

    def marks(s, size, parts=1, base=0):
        held = [entry(link, s) for link in range(3)]
        turn([hits(held[link] // 2, c) for c in range(2) for link in range(3)])
        for q in range(parts):
            for group in range(6):
                first = pl.multiple_of(held[group % 3] % 2 * half + q * size, size)
                spread(group, first, size, base + (q * 6 + group) * size)

    barrier = pltpu.get_barrier_semaphore()
    for to in ("x", "y", "in", "pair"):
        pl.semaphore_signal(barrier, inc=1, device_id=target[to], device_id_type=MESH)

    @pl.when(inner == 1)
    def _():
        pl.semaphore_signal(barrier, inc=1, device_id=target["out"], device_id_type=MESH)

    local = pltpu.make_async_copy(x_hbm, mine, s_load.at[0])
    local_ids = pltpu.make_async_copy(ids_hbm, idb.at[0, core], s_load.at[0])
    load_g = pltpu.make_async_copy(wg_hbm, wg, s_load.at[1])
    load_u = pltpu.make_async_copy(wu_hbm, wu, s_load.at[1])
    load_e = pltpu.make_async_copy(e_hbm, error, s_load.at[1])
    local.start()
    local_ids.start()
    local.wait()
    local_ids.wait()
    pl.semaphore_wait(barrier, 4 + inner)

    roles = ((CORNER, inner == 0), (MIDDLE, inner == 1))
    for role, here in roles:
        @pl.when(here)
        def _():
            for item in sends(role, -1):
                [copy.start() for copy in send_copies(role, item)]

    pair_ids(1, 0).start()
    pair_own.start()
    load_g.start()
    load_u.start()
    wait_ids(s_partid.at[1], 1)
    theirs = own.at[pl.ds((1 - core) * rows, rows), :]
    remote(theirs, theirs, s_send.at[4], s_part.at[1], "pair").wait_recv()
    load_g.wait()
    load_u.wait()
    load_e.start()
    turn([hits(0, c) for c in range(2)])
    for c in range(2):
        spread(c, 0, rows, c * rows)
    hidden(own[...], 2 * rows, 0)
    gram(2 * rows, True)

    def drain(role):
        items = [item for step in range(-1, STEPS) for item in sends(role, step)]
        count = sum(half for item in items if item[2] is not None)
        pairs = sum(size_of(arrivals(role, step)[0]) for step in range(STEPS + 1))
        for n, total in ((0, count), (2, pairs)):
            for view in counted(total):
                remote(view, view, s_send.at[n], s_part.at[0], "pair").wait_send()
        for n, total in ((1, sum(item[2] is None for item in items)), (3, 16)):
            whole, rest = total // 2, total % 2
            for view in [idb.at[pl.ds(0, whole)]] + [idb.at[0, 0]] * rest:
                remote(view, view, s_send.at[n], s_part.at[0], "pair").wait_send()
        pair_own.wait_send()

    def take(role, step):
        filled, ids = arrivals(role, step)
        if step == 0:
            wait_ids(s_idr.at[step], len(ids))
        wait_rows(s_recv.at[step], size_of(filled))
        for item in sends(role, step):
            for copy in send_copies(role, item):
                copy.start()
        if step == 0:
            for j, k in ids:
                pair_ids(step, number(j, k)).start()
        for slot in filled:
            pair_piece(step, slot).start()
        if step and ids:
            wait_ids(s_idr.at[step], len(ids))
            for j, k in ids:
                pair_ids(step, number(j, k)).start()

    def join(role, step):
        filled, ids = arrivals(role, step)
        wait_ids(s_partid.at[step % 2], len(ids))
        wait_rows(s_part.at[step % 2], size_of(filled))

    def when_role(act, *args):
        for role, here in roles:
            @pl.when(here)
            def _():
                act(role, *args)

    def at_step(act, s, steps):
        for role, here in roles:
            for step in steps:
                @pl.when(jnp.logical_and(here, s == step))
                def _():
                    act(role, step)

    full = range(STEPS - 2)

    def loop(s, carry):
        at_step(take, s, full)

        @pl.when(s > 0)
        def _():
            gram(lot, False, pl.multiple_of((s + 1) % 2 * lot, lot))

        @pl.when(s == 1)
        def _():
            load_e.wait()

            def narrow(n, carry):
                some = pl.ds(pl.multiple_of(n * LANES, LANES), LANES)
                error_ref[some, :] = error[some, :].astype(jnp.bfloat16)
                return carry

            lax.fori_loop(0, features // LANES, narrow, 0)

        at_step(join, s, full)

        @pl.when(s == 0)
        def _():
            marks(0, half)

        hidden(tok[s], lot, pl.multiple_of((s % 2) * lot, lot))
        marks(s + 1, half)
        return carry

    lax.fori_loop(0, STEPS - 2, loop, 0)
    last = STEPS - 1
    part = 6 * quarter
    def side(c, s, q, base, between=None, after=1):
        count = lot // 2 if q is None else part // 2
        skip = 0 if q is None else q * part
        rows_at = pl.multiple_of(skip + c * count, count)
        hidden(
            tok[s, pl.ds(rows_at, count), :], count, pl.multiple_of(base + rows_at, count),
            pl.multiple_of(base + rows_at, count), between, after,
        )

    when_role(take, last - 1)
    side(core, last - 1, None, 0)
    gram(lot, False, lot)
    when_role(join, last - 1)
    marks(last, quarter, 2, lot)
    side(1 - core, last - 1, None, 0, lambda: when_role(take, last), 0)
    gram(lot, False)
    when_role(join, last)
    hidden(tok[last, pl.ds(0, part), :], part, lot, lot, lambda: when_role(take, last + 1), 1)
    side(core, last, 1, lot)
    when_role(join, last + 1)
    side(1 - core, last, 1, lot)
    share = 1.0 / jnp.sum((idb[...] == expert).astype(jnp.float32))
    for n in range(bands):
        for m in range(n, bands):
            down, across = pl.ds(n * band, band), pl.ds(m * band, band)
            part = acc[down, across] + lax.dot_general(
                hid[pl.ds(lot, lot), down], hid[pl.ds(lot, lot), across],
                (((0,), (0,)), ((), ())), preferred_element_type=jnp.float32,
            )
            part = part * share
            out_ref[down, across] = part.astype(out_ref.dtype)
            if m > n:
                out_ref[across, down] = part.T.astype(out_ref.dtype)
    when_role(drain)


def finish_kernel(gram_ref, error_ref, out_hbm, done, sem):
    turns, features, cols = done.shape
    tall = features // 3
    blocks = [(n, first) for first in range(0, features, tall) for n in range(turns)]

    def put(at, n, first):
        return pltpu.make_async_copy(
            done.at[n, pl.ds(first, tall), :], out_hbm.at[pl.ds(first, tall), pl.ds(n * cols, cols)], sem.at[at]
        )

    for at, (n, first) in enumerate(blocks):
        done[n, pl.ds(first, tall), :] = jnp.dot(
            gram_ref[pl.ds(first, tall), :], error_ref[:, pl.ds(n * cols, cols)],
            preferred_element_type=jnp.float32,
        )
        put(at, n, first).start()
    for at, block in enumerate(blocks):
        put(at, *block).wait()


def fused_local(tokens, expert_ids, w_gate, w_up, down_error):
    rows, width = tokens.shape
    top = expert_ids.shape[1]
    features = w_gate.shape[2]
    vmem = pl.BlockSpec(memory_space=pltpu.VMEM)
    hbm = pl.BlockSpec(memory_space=pltpu.HBM)
    dma = pltpu.SemaphoreType.DMA
    mean_gram, narrow_error = pl.pallas_call(
        gather_kernel,
        out_shape=(
            jax.ShapeDtypeStruct((features, features), jnp.bfloat16),
            jax.ShapeDtypeStruct((features, width), jnp.bfloat16),
        ),
        in_specs=[hbm] * 5,
        out_specs=(vmem, vmem),
        scratch_shapes=[
            pltpu.VMEM((2 * rows, width), jnp.bfloat16),
            pltpu.VMEM((STEPS, 3 * rows, width), jnp.bfloat16),
            pltpu.VMEM((16, 2, top, rows), jnp.int32),
            pltpu.VMEM((width, features), jnp.bfloat16),
            pltpu.VMEM((width, features), jnp.bfloat16),
            pltpu.VMEM((6 * rows, features), jnp.bfloat16),
            pltpu.VMEM((features, features), jnp.float32),
            pltpu.VMEM((features, width), jnp.float32),
            pltpu.VMEM((rows, 8), jnp.float32),
            pltpu.VMEM((6 * rows, LANES), jnp.float32),
            dma((5,)), dma((STEPS + 1,)), dma((STEPS,)), dma((2,)), dma((2,)), dma((2,)),
        ],
        compiler_params=pltpu.CompilerParams(
            collective_id=0, has_side_effects=True, vmem_limit_bytes=VMEM_LIMIT
        ),
    )(*[
        pltpu.with_memory_space_constraint(a, pltpu.HBM)
        for a in (tokens, expert_ids.T, w_gate[0], w_up[0], down_error[0])
    ])
    return pl.pallas_call(
        finish_kernel,
        out_shape=jax.ShapeDtypeStruct(down_error.shape[1:], jnp.float32),
        in_specs=[vmem, vmem],
        out_specs=hbm,
        scratch_shapes=[pltpu.VMEM((down_error.shape[2] // FINISH_COLS, features, FINISH_COLS), jnp.float32), dma((3 * (down_error.shape[2] // FINISH_COLS),))],
        compiler_params=pltpu.CompilerParams(vmem_limit_bytes=FINISH_LIMIT),
    )(mean_gram, narrow_error)[None]


def hidden_rows(received, w_gate, w_up):
    sources, slots, width = received.shape
    flat_rows = received.reshape(sources * slots, width)
    gate = jnp.dot(flat_rows, w_gate[0], preferred_element_type=jnp.float32)
    upward = jnp.dot(flat_rows, w_up[0], preferred_element_type=jnp.float32)
    hidden = (jax.nn.silu(gate) * upward).astype(jnp.bfloat16)
    return hidden.reshape(sources, slots, hidden.shape[1])


def cross_gram(first, second):
    return lax.dot_general(
        first, second, (((0,), (0,)), ((), ())), preferred_element_type=jnp.float32
    )


def gram_of(hidden):
    middle = hidden.shape[1] // 2
    left_part = hidden[:, :middle]
    right_part = hidden[:, middle:]
    upper_left = cross_gram(left_part, left_part)
    upper_right = cross_gram(left_part, right_part)
    lower_right = cross_gram(right_part, right_part)
    top_band = jnp.concatenate([upper_left, upper_right], axis=1)
    bottom_band = jnp.concatenate([upper_right.T, lower_right], axis=1)
    return jnp.concatenate([top_band, bottom_band], axis=0)


def local(tokens, expert_ids, w_gate, w_up, down_error):
    across = lax.axis_size("gx")
    within = lax.axis_size("gy")
    experts = across * within
    tok_count, top_count = expert_ids.shape
    width = tokens.shape[1]
    assigned = tok_count * top_count
    capacity = 3 * assigned // experts
    flat_ids = expert_ids.reshape(assigned)
    onehot = (flat_ids[:, None] == jnp.arange(experts, dtype=jnp.int32)[None, :]).astype(
        jnp.bfloat16
    )
    positions = jnp.arange(assigned, dtype=jnp.int32)
    lower = (positions[:, None] >= positions[None, :]).astype(jnp.bfloat16)
    running = jnp.dot(lower, onehot, preferred_element_type=jnp.float32)
    slot_of = (jnp.sum(running * onehot, axis=1) - 1.0).astype(jnp.int32)
    target = flat_ids * capacity + slot_of
    picked = tokens[positions // top_count]
    outgoing = jnp.zeros((experts * capacity, width), jnp.bfloat16).at[target].set(picked)
    tallies = jnp.sum(onehot.astype(jnp.float32), axis=0)
    loads = lax.psum_scatter(tallies, ("gx", "gy"), scatter_dimension=0, tiled=True)
    hidden = hidden_rows(
        lax.all_to_all(
            outgoing.reshape(experts, capacity, width),
            ("gx", "gy"),
            split_axis=0,
            concat_axis=0,
            tiled=True,
        ),
        w_gate,
        w_up,
    )
    hidden = hidden.reshape(experts * capacity, hidden.shape[2])
    gram = gram_of(hidden)
    mean_gram = gram / loads[0]
    product = jnp.dot(
        mean_gram,
        down_error[0],
        preferred_element_type=jnp.float32,
        precision=lax.Precision.HIGHEST,
    )
    return product[None]


def solution(mesh):
    small = mesh.shape["gx"] == 8 and mesh.shape["gy"] == 4
    return jax.shard_map(
        fused_local if small else local,
        mesh=mesh,
        in_specs=(
            P(("gx", "gy"), None),
            P(("gx", "gy"), None),
            P(("gx", "gy"), None, None),
            P(("gx", "gy"), None, None),
            P(("gx", "gy"), None, None),
        ),
        out_specs=P(("gx", "gy"), None, None),
        check_vma=False,
    )
```

```python
import jax
import jax.numpy as jnp
from jax import lax
from jax.experimental import pallas as pl
from jax.experimental.pallas import tpu as pltpu
from jax.sharding import PartitionSpec as P

MESH = pl.DeviceIdType.MESH
LANES = 128
VMEM_LIMIT = 46000000
FINISH_LIMIT = 16 * 1024 * 1024


STEPS = 10
CORNER, MIDDLE = 0, 1
FIRST = (0, 3, 5, 7)
FINISH_COLS = 512


def place(role, j, k, h):
    if j == 1:
        return FIRST[k] + 1 - h, 0
    if j == 2:
        return FIRST[k] + h, 1
    if j == 3 and k == 0:
        return 2, h
    if role == CORNER:
        if j == 3 and k == 3:
            return 9, h
        first = {(0, 1): 0, (0, 2): 2, (0, 3): 4, (3, 1): 6, (3, 2): 8}[j, k]
        return first + h, 2
    if j == 0 and k == 1:
        return (8, 2) if h == 0 else (9, 0)
    if j == 3 and k == 1:
        return 9, 1 + h
    first = {(0, 2): 0, (0, 3): 2, (3, 2): 4, (3, 3): 6}[j, k]
    return first + h, 2


def arrival(role, j, k, h):
    if role == MIDDLE and k == 1 and j in (0, 3):
        return h if j == 0 else 4 + h
    return place(role, j, k, h)[0]


def blocks():
    return [(j, k) for j in range(4) for k in range(4) if (j, k) != (0, 0)]


def ids_arrival(role, j, k):
    return max(0, min(arrival(role, j, k, h) for h in range(2)) - 1)


def arrivals(role, step):
    filled = []
    for j, k in blocks():
        for h in range(2):
            (s, link), come = place(role, j, k, h), arrival(role, j, k, h)
            for q in (0, 1) if s == STEPS - 1 else (None,):
                if step == (come + q if come == STEPS - 1 else come):
                    filled.append((s, link, q))
    ids = [(j, k) for j, k in blocks() if ids_arrival(role, j, k) == step]
    return filled, ids


def sends(role, step):
    out = []

    def put(queue, block, halves, there, ids=True):
        if ids:
            out.append((queue, block, None, there))
        out.extend((queue, block, h, there) for h in halves)

    if step < 0:
        put("x", (0, 0), (1, 0), (1, 0))
        put("y", (0, 0), (0, 1), (2, 0))
        put("in", (0, 0), (0, 1), (0, 1) if role == CORNER else (0, 2))
        if role == MIDDLE:
            put("out", (0, 0), (0, 1), (0, 1))
        nth = {item: sum(other[0] == item[0] for other in out[:n]) for n, item in enumerate(out)}
        out.sort(key=nth.get)
    if step == 0:
        put("x", (2, 0), (0,), (3, 0))
        put("y", (1, 0), (1,), (3, 0), ids=False)
    columns = {1: (1,), 3: (2,), 5: (3,)} if role == CORNER else {1: (1, 2), 3: (3,)}
    for k in columns.get(step, ()):
        put("x", (0, k), (1, 0), (1, k))
        put("y", (0, k), (0, 1), (2, k))
    if role == CORNER:
        if step == 2:
            put("in", (3, 0), (0, 1), (3, 1))
        if step == 7:
            put("x", (2, 3), (0,), (3, 3), ids=False)
            put("y", (1, 3), (1,), (3, 3))
        return out
    if step in (0, 1):
        put("out", (0, 2), (step,), (0, 2), ids=step == 0)
        put("in", (0, 1), (step,), (0, 3), ids=step == 0)
    if step == 2:
        put("out", (0, 3), (0,), (0, 3))
        put("in", (3, 0), (0, 1), (3, 2))
    if step == 3:
        put("out", (0, 3), (1,), (0, 3), ids=False)
        put("out", (3, 0), (0, 1), (3, 1))
    if step in (4, 5):
        put("out", (3, 2), (step - 4,), (3, 2), ids=step == 4)
        put("in", (3, 1), (step - 4,), (3, 3), ids=step == 4)
    return out


def receiver(role, queue):
    if queue in ("x", "y"):
        return role
    return CORNER if queue == "out" else MIDDLE


def packed_tables():
    words = []
    for role in (CORNER, MIDDLE):
        held = {place(role, j, k, h): (j * 4 + k) * 2 + h for j, k in blocks() for h in range(2)}
        words.append([
            [sum(held[s, link] << (5 * (s % 6)) for s in range(first, min(first + 6, STEPS))) for first in (0, 6)]
            for link in range(3)
        ])
    return words


def gather_kernel(
    x_hbm, ids_hbm, wg_hbm, wu_hbm, e_hbm, out_ref, error_ref,
    own, tok, idb, wg, wu, hid, acc, error, turned, mask,
    s_send, s_recv, s_idr, s_part, s_partid, s_load,
):
    gx = lax.axis_index("gx")
    z = lax.axis_index("gy")
    rows, width = x_hbm.shape
    half = rows // 2
    quarter = rows // 4
    lot = 3 * rows
    core = gx % 2
    px = (gx // 2) % 2
    py = gx // 4
    expert = gx * 4 + z
    mirror = z // 2
    inner = z + (3 - 2 * z) * mirror

    def dev(a, b, c):
        return b * 4 + a * 2 + c

    inward = z + 1 - 2 * mirror
    target = {
        "x": (dev(1 - px, py, core), z),
        "y": (dev(px, 1 - py, core), z),
        "in": (gx, inward),
        "out": (gx, z - 1 + 2 * mirror),
        "pair": (dev(px, py, 1 - core), z),
    }

    def remote(src, dst, ssem, rsem, to):
        return pltpu.make_async_remote_copy(
            src_ref=src, dst_ref=dst, send_sem=ssem, recv_sem=rsem,
            device_id=target[to], device_id_type=MESH,
        )

    def spot(s, link, c, q=None):
        if s < STEPS - 1:
            first, count = ((c * 3 + link) * half, half) if q is None else ((c * 3 + link) * half + q * quarter, quarter)
        else:
            first, count = (q * 6 + c * 3 + link) * quarter, quarter
        return tok.at[s, pl.ds(first, count), :]

    def cuts(*steps):
        return (0, 1) if max(steps) == STEPS - 1 else (None,)

    def number(j, k):
        return j * 4 + k

    def send_copies(role, item):
        queue, (j, k), h, there = item
        far = receiver(role, queue)
        if h is None:
            src, dst = idb.at[number(j, k), core], idb.at[number(*there), core]
            return [remote(src, dst, s_send.at[1], s_idr.at[ids_arrival(far, *there)], queue)]
        s, link = place(far, *there, h)
        come = arrival(far, *there, h)
        mine = None if (j, k) == (0, 0) else place(role, j, k, h)
        copies = []
        for q in cuts(s, 0 if mine is None else mine[0]):
            if mine is not None:
                src = spot(*mine, core, q)
            elif q is None:
                src = own.at[pl.ds(core * rows + h * half, half), :]
            else:
                src = own.at[pl.ds(core * rows + h * half + q * quarter, quarter), :]
            step = come + (q if come == STEPS - 1 else 0)
            copies.append(remote(src, spot(s, link, core, q), s_send.at[0], s_recv.at[step], queue))
        return copies

    def pair_piece(step, slot):
        return remote(spot(*slot[:2], core, slot[2]), spot(*slot[:2], core, slot[2]), s_send.at[2], s_part.at[step % 2], "pair")

    def pair_ids(step, b):
        return remote(idb.at[b, core], idb.at[b, core], s_send.at[3], s_partid.at[step % 2], "pair")

    mine = own.at[pl.ds(core * rows, rows), :]
    pair_own = remote(mine, mine, s_send.at[4], s_part.at[1], "pair")

    def size_of(filled):
        return sum(half if q is None else quarter for _, _, q in filled)

    def counted(count):
        views = [tok.at[pl.ds(0, count // lot)]] if count >= lot else []
        return views + ([tok.at[0, pl.ds(0, count % lot), :]] if count % lot else [])

    def wait_rows(sem, count):
        for view in counted(count):
            remote(view, view, s_send.at[0], sem, "pair").wait_recv()

    def wait_ids(sem, count):
        if count:
            view = idb.at[pl.ds(0, count), 0]
            remote(view, view, s_send.at[0], sem, "pair").wait_recv()

    bands = 3
    features = hid.shape[1]
    band = features // bands

    def hits(b, c):
        return jnp.sum((idb[b, c] == expert).astype(jnp.float32), axis=0, keepdims=True)

    def turn(rows_of):
        spare = jnp.zeros((8 - len(rows_of), rows), jnp.float32)
        turned[...] = jnp.concatenate(rows_of + [spare], axis=0).T

    def spread(group, first, count, to):
        mask[pl.ds(to, count), :] = jnp.broadcast_to(turned[pl.ds(first, count), group:group + 1], (count, LANES))

    def hidden(rows_in, count, base, first=0, between=None, after=1):
        live = jnp.concatenate([mask[pl.ds(first, count), :]] * (band // LANES), axis=1)
        for n in range(bands):
            cols = pl.ds(n * band, band)
            gate = jnp.dot(rows_in, wg[:, cols], preferred_element_type=jnp.float32)
            upward = jnp.dot(rows_in, wu[:, cols], preferred_element_type=jnp.float32)
            value = gate / (1.0 + jnp.exp(-gate)) * upward
            hid[pl.ds(base, count), cols] = jnp.where(live > 0.5, value, 0.0).astype(jnp.bfloat16)
            if between is not None and n == after:
                between()

    def gram(count, start, base=0):
        for n in range(bands):
            rest = pl.ds(n * band, features - n * band)
            part = lax.dot_general(
                hid[pl.ds(base, count), pl.ds(n * band, band)], hid[pl.ds(base, count), rest],
                (((0,), (0,)), ((), ())), preferred_element_type=jnp.float32,
            )
            if start:
                acc[pl.ds(n * band, band), rest] = part
            else:
                acc[pl.ds(n * band, band), rest] += part

    tables = packed_tables()

    def entry(link, s):
        corner, middle = tables[CORNER][link], tables[MIDDLE][link]
        low = corner[0] + (middle[0] - corner[0]) * inner
        high = corner[1] + (middle[1] - corner[1]) * inner
        word = low + (high - low) * (s // 6)
        return (word >> (5 * (s % 6))) % 32

    def marks(s, size, parts=1, base=0):
        held = [entry(link, s) for link in range(3)]
        turn([hits(held[link] // 2, c) for c in range(2) for link in range(3)])
        for q in range(parts):
            for group in range(6):
                first = pl.multiple_of(held[group % 3] % 2 * half + q * size, size)
                spread(group, first, size, base + (q * 6 + group) * size)

    barrier = pltpu.get_barrier_semaphore()
    for to in ("x", "y", "in", "pair"):
        pl.semaphore_signal(barrier, inc=1, device_id=target[to], device_id_type=MESH)

    @pl.when(inner == 1)
    def _():
        pl.semaphore_signal(barrier, inc=1, device_id=target["out"], device_id_type=MESH)

    local = pltpu.make_async_copy(x_hbm, mine, s_load.at[0])
    local_ids = pltpu.make_async_copy(ids_hbm, idb.at[0, core], s_load.at[0])
    load_g = pltpu.make_async_copy(wg_hbm, wg, s_load.at[1])
    load_u = pltpu.make_async_copy(wu_hbm, wu, s_load.at[1])
    load_e = pltpu.make_async_copy(e_hbm, error, s_load.at[1])
    local.start()
    local_ids.start()
    local.wait()
    local_ids.wait()
    pl.semaphore_wait(barrier, 4 + inner)

    roles = ((CORNER, inner == 0), (MIDDLE, inner == 1))
    for role, here in roles:
        @pl.when(here)
        def _():
            for item in sends(role, -1):
                [copy.start() for copy in send_copies(role, item)]

    pair_ids(1, 0).start()
    pair_own.start()
    load_g.start()
    load_u.start()
    wait_ids(s_partid.at[1], 1)
    theirs = own.at[pl.ds((1 - core) * rows, rows), :]
    remote(theirs, theirs, s_send.at[4], s_part.at[1], "pair").wait_recv()
    load_g.wait()
    load_u.wait()
    load_e.start()
    turn([hits(0, c) for c in range(2)])
    for c in range(2):
        spread(c, 0, rows, c * rows)
    hidden(own[...], 2 * rows, 0)
    gram(2 * rows, True)

    def drain(role):
        items = [item for step in range(-1, STEPS) for item in sends(role, step)]
        count = sum(half for item in items if item[2] is not None)
        pairs = sum(size_of(arrivals(role, step)[0]) for step in range(STEPS + 1))
        for n, total in ((0, count), (2, pairs)):
            for view in counted(total):
                remote(view, view, s_send.at[n], s_part.at[0], "pair").wait_send()
        for n, total in ((1, sum(item[2] is None for item in items)), (3, 16)):
            whole, rest = total // 2, total % 2
            for view in [idb.at[pl.ds(0, whole)]] + [idb.at[0, 0]] * rest:
                remote(view, view, s_send.at[n], s_part.at[0], "pair").wait_send()
        pair_own.wait_send()

    def take(role, step):
        filled, ids = arrivals(role, step)
        if step == 0:
            wait_ids(s_idr.at[step], len(ids))
        wait_rows(s_recv.at[step], size_of(filled))
        for item in sends(role, step):
            for copy in send_copies(role, item):
                copy.start()
        if step == 0:
            for j, k in ids:
                pair_ids(step, number(j, k)).start()
        for slot in filled:
            pair_piece(step, slot).start()
        if step and ids:
            wait_ids(s_idr.at[step], len(ids))
            for j, k in ids:
                pair_ids(step, number(j, k)).start()

    def join(role, step):
        filled, ids = arrivals(role, step)
        wait_ids(s_partid.at[step % 2], len(ids))
        wait_rows(s_part.at[step % 2], size_of(filled))

    def when_role(act, *args):
        for role, here in roles:
            @pl.when(here)
            def _():
                act(role, *args)

    def at_step(act, s, steps):
        for role, here in roles:
            for step in steps:
                @pl.when(jnp.logical_and(here, s == step))
                def _():
                    act(role, step)

    full = range(STEPS - 2)

    def loop(s, carry):
        at_step(take, s, full)

        @pl.when(s > 0)
        def _():
            gram(lot, False, pl.multiple_of((s + 1) % 2 * lot, lot))

        @pl.when(s == 1)
        def _():
            load_e.wait()

            def narrow(n, carry):
                some = pl.ds(pl.multiple_of(n * LANES, LANES), LANES)
                error_ref[some, :] = error[some, :].astype(jnp.bfloat16)
                return carry

            lax.fori_loop(0, features // LANES, narrow, 0)

        at_step(join, s, full)

        @pl.when(s == 0)
        def _():
            marks(0, half)

        hidden(tok[s], lot, pl.multiple_of((s % 2) * lot, lot))
        marks(s + 1, half)
        return carry

    lax.fori_loop(0, STEPS - 2, loop, 0)
    last = STEPS - 1
    part = 6 * quarter
    def side(c, s, q, base, between=None, after=1):
        count = lot // 2 if q is None else part // 2
        skip = 0 if q is None else q * part
        rows_at = pl.multiple_of(skip + c * count, count)
        hidden(
            tok[s, pl.ds(rows_at, count), :], count, pl.multiple_of(base + rows_at, count),
            pl.multiple_of(base + rows_at, count), between, after,
        )

    when_role(take, last - 1)
    side(core, last - 1, None, 0)
    gram(lot, False, lot)
    when_role(join, last - 1)
    marks(last, quarter, 2, lot)
    side(1 - core, last - 1, None, 0, lambda: when_role(take, last), 0)
    gram(lot, False)
    when_role(join, last)
    hidden(tok[last, pl.ds(0, part), :], part, lot, lot, lambda: when_role(take, last + 1), 1)
    side(core, last, 1, lot)
    when_role(join, last + 1)
    side(1 - core, last, 1, lot)
    share = 1.0 / jnp.sum((idb[...] == expert).astype(jnp.float32))
    for n in range(bands):
        for m in range(n, bands):
            down, across = pl.ds(n * band, band), pl.ds(m * band, band)
            part = acc[down, across] + lax.dot_general(
                hid[pl.ds(lot, lot), down], hid[pl.ds(lot, lot), across],
                (((0,), (0,)), ((), ())), preferred_element_type=jnp.float32,
            )
            part = part * share
            out_ref[down, across] = part.astype(out_ref.dtype)
            if m > n:
                out_ref[across, down] = part.T.astype(out_ref.dtype)
    when_role(drain)


def finish_kernel(gram_ref, error_ref, out_hbm, done, sem):
    turns, features, cols = done.shape
    tall = features // 3
    blocks = [(n, first) for first in range(0, features, tall) for n in range(turns)]

    for n, first in blocks:
        done[n, pl.ds(first, tall), :] = jnp.dot(
            gram_ref[pl.ds(first, tall), :], error_ref[:, pl.ds(n * cols, cols)],
            preferred_element_type=jnp.float32,
        )
        pltpu.make_async_copy(
            done.at[n, pl.ds(first, tall), :], out_hbm.at[pl.ds(first, tall), pl.ds(n * cols, cols)], sem.at[0]
        ).start()
    pltpu.make_async_copy(done, done, sem.at[0]).wait()


def fused_local(tokens, expert_ids, w_gate, w_up, down_error):
    rows, width = tokens.shape
    top = expert_ids.shape[1]
    features = w_gate.shape[2]
    vmem = pl.BlockSpec(memory_space=pltpu.VMEM)
    hbm = pl.BlockSpec(memory_space=pltpu.HBM)
    dma = pltpu.SemaphoreType.DMA
    mean_gram, narrow_error = pl.pallas_call(
        gather_kernel,
        out_shape=(
            jax.ShapeDtypeStruct((features, features), jnp.bfloat16),
            jax.ShapeDtypeStruct((features, width), jnp.bfloat16),
        ),
        in_specs=[hbm] * 5,
        out_specs=(vmem, vmem),
        scratch_shapes=[
            pltpu.VMEM((2 * rows, width), jnp.bfloat16),
            pltpu.VMEM((STEPS, 3 * rows, width), jnp.bfloat16),
            pltpu.VMEM((16, 2, top, rows), jnp.int32),
            pltpu.VMEM((width, features), jnp.bfloat16),
            pltpu.VMEM((width, features), jnp.bfloat16),
            pltpu.VMEM((6 * rows, features), jnp.bfloat16),
            pltpu.VMEM((features, features), jnp.float32),
            pltpu.VMEM((features, width), jnp.float32),
            pltpu.VMEM((rows, 8), jnp.float32),
            pltpu.VMEM((6 * rows, LANES), jnp.float32),
            dma((5,)), dma((STEPS + 1,)), dma((STEPS,)), dma((2,)), dma((2,)), dma((2,)),
        ],
        compiler_params=pltpu.CompilerParams(
            collective_id=0, has_side_effects=True, vmem_limit_bytes=VMEM_LIMIT
        ),
    )(*[
        pltpu.with_memory_space_constraint(a, pltpu.HBM)
        for a in (tokens, expert_ids.T, w_gate[0], w_up[0], down_error[0])
    ])
    return pl.pallas_call(
        finish_kernel,
        out_shape=jax.ShapeDtypeStruct(down_error.shape[1:], jnp.float32),
        in_specs=[vmem, vmem],
        out_specs=hbm,
        scratch_shapes=[pltpu.VMEM((down_error.shape[2] // FINISH_COLS, features, FINISH_COLS), jnp.float32), dma((1,))],
        compiler_params=pltpu.CompilerParams(vmem_limit_bytes=FINISH_LIMIT),
    )(mean_gram, narrow_error)[None]


def hidden_rows(received, w_gate, w_up):
    sources, slots, width = received.shape
    flat_rows = received.reshape(sources * slots, width)
    gate = jnp.dot(flat_rows, w_gate[0], preferred_element_type=jnp.float32)
    upward = jnp.dot(flat_rows, w_up[0], preferred_element_type=jnp.float32)
    hidden = (jax.nn.silu(gate) * upward).astype(jnp.bfloat16)
    return hidden.reshape(sources, slots, hidden.shape[1])


def cross_gram(first, second):
    return lax.dot_general(
        first, second, (((0,), (0,)), ((), ())), preferred_element_type=jnp.float32
    )


def gram_of(hidden):
    middle = hidden.shape[1] // 2
    left_part = hidden[:, :middle]
    right_part = hidden[:, middle:]
    upper_left = cross_gram(left_part, left_part)
    upper_right = cross_gram(left_part, right_part)
    lower_right = cross_gram(right_part, right_part)
    top_band = jnp.concatenate([upper_left, upper_right], axis=1)
    bottom_band = jnp.concatenate([upper_right.T, lower_right], axis=1)
    return jnp.concatenate([top_band, bottom_band], axis=0)


def local(tokens, expert_ids, w_gate, w_up, down_error):
    across = lax.axis_size("gx")
    within = lax.axis_size("gy")
    experts = across * within
    tok_count, top_count = expert_ids.shape
    width = tokens.shape[1]
    assigned = tok_count * top_count
    capacity = 3 * assigned // experts
    flat_ids = expert_ids.reshape(assigned)
    onehot = (flat_ids[:, None] == jnp.arange(experts, dtype=jnp.int32)[None, :]).astype(
        jnp.bfloat16
    )
    positions = jnp.arange(assigned, dtype=jnp.int32)
    lower = (positions[:, None] >= positions[None, :]).astype(jnp.bfloat16)
    running = jnp.dot(lower, onehot, preferred_element_type=jnp.float32)
    slot_of = (jnp.sum(running * onehot, axis=1) - 1.0).astype(jnp.int32)
    target = flat_ids * capacity + slot_of
    picked = tokens[positions // top_count]
    outgoing = jnp.zeros((experts * capacity, width), jnp.bfloat16).at[target].set(picked)
    tallies = jnp.sum(onehot.astype(jnp.float32), axis=0)
    loads = lax.psum_scatter(tallies, ("gx", "gy"), scatter_dimension=0, tiled=True)
    hidden = hidden_rows(
        lax.all_to_all(
            outgoing.reshape(experts, capacity, width),
            ("gx", "gy"),
            split_axis=0,
            concat_axis=0,
            tiled=True,
        ),
        w_gate,
        w_up,
    )
    hidden = hidden.reshape(experts * capacity, hidden.shape[2])
    gram = gram_of(hidden)
    mean_gram = gram / loads[0]
    product = jnp.dot(
        mean_gram,
        down_error[0],
        preferred_element_type=jnp.float32,
        precision=lax.Precision.HIGHEST,
    )
    return product[None]


def solution(mesh):
    small = mesh.shape["gx"] == 8 and mesh.shape["gy"] == 4
    return jax.shard_map(
        fused_local if small else local,
        mesh=mesh,
        in_specs=(
            P(("gx", "gy"), None),
            P(("gx", "gy"), None),
            P(("gx", "gy"), None, None),
            P(("gx", "gy"), None, None),
            P(("gx", "gy"), None, None),
        ),
        out_specs=P(("gx", "gy"), None, None),
        check_vma=False,
    )
```

```python
import jax
import jax.numpy as jnp
from jax import lax
from jax.experimental import pallas as pl
from jax.experimental.pallas import tpu as pltpu
from jax.sharding import PartitionSpec as P

MESH = pl.DeviceIdType.MESH
LANES = 128
VMEM_LIMIT = 46000000
FINISH_LIMIT = 16 * 1024 * 1024


STEPS = 10
CORNER, MIDDLE = 0, 1
FIRST = (0, 3, 5, 7)
FINISH_COLS = 512


def place(role, j, k, h):
    if j == 1:
        return FIRST[k] + 1 - h, 0
    if j == 2:
        return FIRST[k] + h, 1
    if j == 3 and k == 0:
        return 2, h
    if role == CORNER:
        if j == 3 and k == 3:
            return 9, h
        first = {(0, 1): 0, (0, 2): 2, (0, 3): 4, (3, 1): 6, (3, 2): 8}[j, k]
        return first + h, 2
    if j == 0 and k == 1:
        return (8, 2) if h == 0 else (9, 0)
    if j == 3 and k == 1:
        return 9, 1 + h
    first = {(0, 2): 0, (0, 3): 2, (3, 2): 4, (3, 3): 6}[j, k]
    return first + h, 2


def arrival(role, j, k, h):
    if role == MIDDLE and k == 1 and j in (0, 3):
        return h if j == 0 else 4 + h
    return place(role, j, k, h)[0]


def blocks():
    return [(j, k) for j in range(4) for k in range(4) if (j, k) != (0, 0)]


def ids_arrival(role, j, k):
    return max(0, min(arrival(role, j, k, h) for h in range(2)) - 1)


def arrivals(role, step):
    filled = []
    for j, k in blocks():
        for h in range(2):
            (s, link), come = place(role, j, k, h), arrival(role, j, k, h)
            for q in (0, 1) if s == STEPS - 1 else (None,):
                if step == (come + q if come == STEPS - 1 else come):
                    filled.append((s, link, q))
    ids = [(j, k) for j, k in blocks() if ids_arrival(role, j, k) == step]
    return filled, ids


def sends(role, step):
    out = []

    def put(queue, block, halves, there, ids=True):
        if ids:
            out.append((queue, block, None, there))
        out.extend((queue, block, h, there) for h in halves)

    if step < 0:
        put("x", (0, 0), (1, 0), (1, 0))
        put("y", (0, 0), (0, 1), (2, 0))
        put("in", (0, 0), (0, 1), (0, 1) if role == CORNER else (0, 2))
        if role == MIDDLE:
            put("out", (0, 0), (0, 1), (0, 1))
        nth = {item: sum(other[0] == item[0] for other in out[:n]) for n, item in enumerate(out)}
        out.sort(key=nth.get)
    if step == 0:
        put("x", (2, 0), (0,), (3, 0))
        put("y", (1, 0), (1,), (3, 0), ids=False)
    columns = {1: (1,), 3: (2,), 5: (3,)} if role == CORNER else {1: (1, 2), 3: (3,)}
    for k in columns.get(step, ()):
        put("x", (0, k), (1, 0), (1, k))
        put("y", (0, k), (0, 1), (2, k))
    if role == CORNER:
        if step == 2:
            put("in", (3, 0), (0, 1), (3, 1))
        if step == 7:
            put("x", (2, 3), (0,), (3, 3), ids=False)
            put("y", (1, 3), (1,), (3, 3))
        return out
    if step in (0, 1):
        put("out", (0, 2), (step,), (0, 2), ids=step == 0)
        put("in", (0, 1), (step,), (0, 3), ids=step == 0)
    if step == 2:
        put("out", (0, 3), (0,), (0, 3))
        put("in", (3, 0), (0, 1), (3, 2))
    if step == 3:
        put("out", (0, 3), (1,), (0, 3), ids=False)
        put("out", (3, 0), (0, 1), (3, 1))
    if step in (4, 5):
        put("out", (3, 2), (step - 4,), (3, 2), ids=step == 4)
        put("in", (3, 1), (step - 4,), (3, 3), ids=step == 4)
    return out


def receiver(role, queue):
    if queue in ("x", "y"):
        return role
    return CORNER if queue == "out" else MIDDLE


def packed_tables():
    words = []
    for role in (CORNER, MIDDLE):
        held = {place(role, j, k, h): (j * 4 + k) * 2 + h for j, k in blocks() for h in range(2)}
        words.append([
            [sum(held[s, link] << (5 * (s % 6)) for s in range(first, min(first + 6, STEPS))) for first in (0, 6)]
            for link in range(3)
        ])
    return words


def gather_kernel(
    x_hbm, ids_hbm, wg_hbm, wu_hbm, e_hbm, out_ref, error_ref,
    own, tok, idb, wg, wu, hid, acc, error, turned, mask,
    s_send, s_recv, s_idr, s_part, s_partid, s_load,
):
    gx = lax.axis_index("gx")
    z = lax.axis_index("gy")
    rows, width = x_hbm.shape
    half = rows // 2
    quarter = rows // 4
    lot = 3 * rows
    core = gx % 2
    px = (gx // 2) % 2
    py = gx // 4
    expert = gx * 4 + z
    mirror = z // 2
    inner = z + (3 - 2 * z) * mirror

    def dev(a, b, c):
        return b * 4 + a * 2 + c

    inward = z + 1 - 2 * mirror
    target = {
        "x": (dev(1 - px, py, core), z),
        "y": (dev(px, 1 - py, core), z),
        "in": (gx, inward),
        "out": (gx, z - 1 + 2 * mirror),
        "pair": (dev(px, py, 1 - core), z),
    }

    def remote(src, dst, ssem, rsem, to):
        return pltpu.make_async_remote_copy(
            src_ref=src, dst_ref=dst, send_sem=ssem, recv_sem=rsem,
            device_id=target[to], device_id_type=MESH,
        )

    def spot(s, link, c, q=None):
        if s < STEPS - 1:
            first, count = ((c * 3 + link) * half, half) if q is None else ((c * 3 + link) * half + q * quarter, quarter)
        else:
            first, count = (q * 6 + c * 3 + link) * quarter, quarter
        return tok.at[s, pl.ds(first, count), :]

    def cuts(*steps):
        return (0, 1) if max(steps) == STEPS - 1 else (None,)

    def number(j, k):
        return j * 4 + k

    def send_copies(role, item):
        queue, (j, k), h, there = item
        far = receiver(role, queue)
        if h is None:
            src, dst = idb.at[number(j, k), core], idb.at[number(*there), core]
            return [remote(src, dst, s_send.at[1], s_idr.at[ids_arrival(far, *there)], queue)]
        s, link = place(far, *there, h)
        come = arrival(far, *there, h)
        mine = None if (j, k) == (0, 0) else place(role, j, k, h)
        copies = []
        for q in cuts(s, 0 if mine is None else mine[0]):
            if mine is not None:
                src = spot(*mine, core, q)
            elif q is None:
                src = own.at[pl.ds(core * rows + h * half, half), :]
            else:
                src = own.at[pl.ds(core * rows + h * half + q * quarter, quarter), :]
            step = come + (q if come == STEPS - 1 else 0)
            copies.append(remote(src, spot(s, link, core, q), s_send.at[0], s_recv.at[step], queue))
        return copies

    def pair_piece(step, slot):
        return remote(spot(*slot[:2], core, slot[2]), spot(*slot[:2], core, slot[2]), s_send.at[2], s_part.at[step % 2], "pair")

    def pair_ids(step, b):
        return remote(idb.at[b, core], idb.at[b, core], s_send.at[3], s_partid.at[step % 2], "pair")

    mine = own.at[pl.ds(core * rows, rows), :]
    pair_own = remote(mine, mine, s_send.at[4], s_part.at[1], "pair")

    def size_of(filled):
        return sum(half if q is None else quarter for _, _, q in filled)

    def counted(count):
        views = [tok.at[pl.ds(0, count // lot)]] if count >= lot else []
        return views + ([tok.at[0, pl.ds(0, count % lot), :]] if count % lot else [])

    def wait_rows(sem, count):
        for view in counted(count):
            remote(view, view, s_send.at[0], sem, "pair").wait_recv()

    def wait_ids(sem, count):
        if count:
            view = idb.at[pl.ds(0, count), 0]
            remote(view, view, s_send.at[0], sem, "pair").wait_recv()

    bands = 3
    features = hid.shape[1]
    band = features // bands

    def hits(b, c):
        return jnp.sum((idb[b, c] == expert).astype(jnp.float32), axis=0, keepdims=True)

    def turn(rows_of):
        spare = jnp.zeros((8 - len(rows_of), rows), jnp.float32)
        turned[...] = jnp.concatenate(rows_of + [spare], axis=0).T

    def spread(group, first, count, to):
        mask[pl.ds(to, count), :] = jnp.broadcast_to(turned[pl.ds(first, count), group:group + 1], (count, LANES))

    def hidden(rows_in, count, base, first=0, between=None, after=1):
        live = jnp.concatenate([mask[pl.ds(first, count), :]] * (band // LANES), axis=1)
        for n in range(bands):
            cols = pl.ds(n * band, band)
            gate = jnp.dot(rows_in, wg[:, cols], preferred_element_type=jnp.float32)
            upward = jnp.dot(rows_in, wu[:, cols], preferred_element_type=jnp.float32)
            value = gate / (1.0 + jnp.exp(-gate)) * upward
            hid[pl.ds(base, count), cols] = jnp.where(live > 0.5, value, 0.0).astype(jnp.bfloat16)
            if between is not None and n == after:
                between()

    def gram(count, start, base=0):
        for n in range(bands):
            rest = pl.ds(n * band, features - n * band)
            part = lax.dot_general(
                hid[pl.ds(base, count), pl.ds(n * band, band)], hid[pl.ds(base, count), rest],
                (((0,), (0,)), ((), ())), preferred_element_type=jnp.float32,
            )
            if start:
                acc[pl.ds(n * band, band), rest] = part
            else:
                acc[pl.ds(n * band, band), rest] += part

    tables = packed_tables()

    def entry(link, s):
        corner, middle = tables[CORNER][link], tables[MIDDLE][link]
        low = corner[0] + (middle[0] - corner[0]) * inner
        high = corner[1] + (middle[1] - corner[1]) * inner
        word = low + (high - low) * (s // 6)
        return (word >> (5 * (s % 6))) % 32

    def marks(s, size, parts=1, base=0):
        held = [entry(link, s) for link in range(3)]
        turn([hits(held[link] // 2, c) for c in range(2) for link in range(3)])
        for q in range(parts):
            for group in range(6):
                first = pl.multiple_of(held[group % 3] % 2 * half + q * size, size)
                spread(group, first, size, base + (q * 6 + group) * size)

    barrier = pltpu.get_barrier_semaphore()
    for to in ("x", "y", "in", "pair"):
        pl.semaphore_signal(barrier, inc=1, device_id=target[to], device_id_type=MESH)

    @pl.when(inner == 1)
    def _():
        pl.semaphore_signal(barrier, inc=1, device_id=target["out"], device_id_type=MESH)

    local = pltpu.make_async_copy(x_hbm, mine, s_load.at[0])
    local_ids = pltpu.make_async_copy(ids_hbm, idb.at[0, core], s_load.at[0])
    load_g = pltpu.make_async_copy(wg_hbm, wg, s_load.at[1])
    load_u = pltpu.make_async_copy(wu_hbm, wu, s_load.at[1])
    load_e = pltpu.make_async_copy(e_hbm, error, s_load.at[1])
    local.start()
    local_ids.start()
    local.wait()
    local_ids.wait()
    pl.semaphore_wait(barrier, 4 + inner)

    roles = ((CORNER, inner == 0), (MIDDLE, inner == 1))
    for role, here in roles:
        @pl.when(here)
        def _():
            for item in sends(role, -1):
                [copy.start() for copy in send_copies(role, item)]

    pair_ids(1, 0).start()
    pair_own.start()
    load_g.start()
    load_u.start()
    wait_ids(s_partid.at[1], 1)
    theirs = own.at[pl.ds((1 - core) * rows, rows), :]
    remote(theirs, theirs, s_send.at[4], s_part.at[1], "pair").wait_recv()
    load_g.wait()
    load_u.wait()
    load_e.start()
    turn([hits(0, c) for c in range(2)])
    for c in range(2):
        spread(c, 0, rows, c * rows)
    hidden(own[...], 2 * rows, 0)
    gram(2 * rows, True)

    def drain(role):
        items = [item for step in range(-1, STEPS) for item in sends(role, step)]
        count = sum(half for item in items if item[2] is not None)
        pairs = sum(size_of(arrivals(role, step)[0]) for step in range(STEPS + 1))
        for n, total in ((0, count), (2, pairs)):
            for view in counted(total):
                remote(view, view, s_send.at[n], s_part.at[0], "pair").wait_send()
        for n, total in ((1, sum(item[2] is None for item in items)), (3, 16)):
            whole, rest = total // 2, total % 2
            for view in [idb.at[pl.ds(0, whole)]] + [idb.at[0, 0]] * rest:
                remote(view, view, s_send.at[n], s_part.at[0], "pair").wait_send()
        pair_own.wait_send()

    def take(role, step):
        filled, ids = arrivals(role, step)
        if step == 0:
            wait_ids(s_idr.at[step], len(ids))
        wait_rows(s_recv.at[step], size_of(filled))
        for item in sends(role, step):
            for copy in send_copies(role, item):
                copy.start()
        if step == 0:
            for j, k in ids:
                pair_ids(step, number(j, k)).start()
        for slot in filled:
            pair_piece(step, slot).start()
        if step and ids:
            wait_ids(s_idr.at[step], len(ids))
            for j, k in ids:
                pair_ids(step, number(j, k)).start()

    def join(role, step):
        filled, ids = arrivals(role, step)
        wait_ids(s_partid.at[step % 2], len(ids))
        wait_rows(s_part.at[step % 2], size_of(filled))

    def when_role(act, *args):
        for role, here in roles:
            @pl.when(here)
            def _():
                act(role, *args)

    def at_step(act, s, steps):
        for role, here in roles:
            for step in steps:
                @pl.when(jnp.logical_and(here, s == step))
                def _():
                    act(role, step)

    full = range(STEPS - 2)

    def loop(s, carry):
        at_step(take, s, full)

        @pl.when(s > 0)
        def _():
            gram(lot, False, pl.multiple_of((s + 1) % 2 * lot, lot))

        @pl.when(s == 1)
        def _():
            load_e.wait()

            def narrow(n, carry):
                some = pl.ds(pl.multiple_of(n * LANES, LANES), LANES)
                error_ref[some, :] = error[some, :].astype(jnp.bfloat16)
                return carry

            lax.fori_loop(0, features // LANES, narrow, 0)

        at_step(join, s, full)

        @pl.when(s == 0)
        def _():
            marks(0, half)

        hidden(tok[s], lot, pl.multiple_of((s % 2) * lot, lot))
        marks(s + 1, half)
        return carry

    lax.fori_loop(0, STEPS - 2, loop, 0)
    last = STEPS - 1
    part = 6 * quarter
    def side(c, s, q, base, between=None, after=1):
        count = lot // 2 if q is None else part // 2
        skip = 0 if q is None else q * part
        rows_at = pl.multiple_of(skip + c * count, count)
        hidden(
            tok[s, pl.ds(rows_at, count), :], count, pl.multiple_of(base + rows_at, count),
            pl.multiple_of(base + rows_at, count), between, after,
        )

    when_role(take, last - 1)
    side(core, last - 1, None, 0)
    gram(lot, False, lot)
    when_role(join, last - 1)
    marks(last, quarter, 2, lot)
    side(1 - core, last - 1, None, 0, lambda: when_role(take, last), 0)
    when_role(join, last)
    hidden(tok[last, pl.ds(0, part), :], part, lot, lot, lambda: when_role(take, last + 1), 1)
    gram(lot, False)
    when_role(join, last + 1)
    hidden(tok[last, pl.ds(part, part), :], part, lot + part, lot + part)
    share = 1.0 / jnp.sum((idb[...] == expert).astype(jnp.float32))
    for n in range(bands):
        for m in range(n, bands):
            down, across = pl.ds(n * band, band), pl.ds(m * band, band)
            part = acc[down, across] + lax.dot_general(
                hid[pl.ds(lot, lot), down], hid[pl.ds(lot, lot), across],
                (((0,), (0,)), ((), ())), preferred_element_type=jnp.float32,
            )
            part = part * share
            out_ref[down, across] = part.astype(out_ref.dtype)
            if m > n:
                out_ref[across, down] = part.T.astype(out_ref.dtype)
    when_role(drain)


def finish_kernel(gram_ref, error_ref, out_hbm, done, sem):
    turns, features, cols = done.shape
    tall = features // 3
    blocks = [(n, first) for first in range(0, features, tall) for n in range(turns)]

    for n, first in blocks:
        done[n, pl.ds(first, tall), :] = jnp.dot(
            gram_ref[pl.ds(first, tall), :], error_ref[:, pl.ds(n * cols, cols)],
            preferred_element_type=jnp.float32,
        )
        pltpu.make_async_copy(
            done.at[n, pl.ds(first, tall), :], out_hbm.at[pl.ds(first, tall), pl.ds(n * cols, cols)], sem.at[0]
        ).start()
    pltpu.make_async_copy(done, done, sem.at[0]).wait()


def fused_local(tokens, expert_ids, w_gate, w_up, down_error):
    rows, width = tokens.shape
    top = expert_ids.shape[1]
    features = w_gate.shape[2]
    vmem = pl.BlockSpec(memory_space=pltpu.VMEM)
    hbm = pl.BlockSpec(memory_space=pltpu.HBM)
    dma = pltpu.SemaphoreType.DMA
    mean_gram, narrow_error = pl.pallas_call(
        gather_kernel,
        out_shape=(
            jax.ShapeDtypeStruct((features, features), jnp.bfloat16),
            jax.ShapeDtypeStruct((features, width), jnp.bfloat16),
        ),
        in_specs=[hbm] * 5,
        out_specs=(vmem, vmem),
        scratch_shapes=[
            pltpu.VMEM((2 * rows, width), jnp.bfloat16),
            pltpu.VMEM((STEPS, 3 * rows, width), jnp.bfloat16),
            pltpu.VMEM((16, 2, top, rows), jnp.int32),
            pltpu.VMEM((width, features), jnp.bfloat16),
            pltpu.VMEM((width, features), jnp.bfloat16),
            pltpu.VMEM((6 * rows, features), jnp.bfloat16),
            pltpu.VMEM((features, features), jnp.float32),
            pltpu.VMEM((features, width), jnp.float32),
            pltpu.VMEM((rows, 8), jnp.float32),
            pltpu.VMEM((6 * rows, LANES), jnp.float32),
            dma((5,)), dma((STEPS + 1,)), dma((STEPS,)), dma((2,)), dma((2,)), dma((2,)),
        ],
        compiler_params=pltpu.CompilerParams(
            collective_id=0, has_side_effects=True, vmem_limit_bytes=VMEM_LIMIT
        ),
    )(*[
        pltpu.with_memory_space_constraint(a, pltpu.HBM)
        for a in (tokens, expert_ids.T, w_gate[0], w_up[0], down_error[0])
    ])
    return pl.pallas_call(
        finish_kernel,
        out_shape=jax.ShapeDtypeStruct(down_error.shape[1:], jnp.float32),
        in_specs=[vmem, vmem],
        out_specs=hbm,
        scratch_shapes=[pltpu.VMEM((down_error.shape[2] // FINISH_COLS, features, FINISH_COLS), jnp.float32), dma((1,))],
        compiler_params=pltpu.CompilerParams(vmem_limit_bytes=FINISH_LIMIT),
    )(mean_gram, narrow_error)[None]


def hidden_rows(received, w_gate, w_up):
    sources, slots, width = received.shape
    flat_rows = received.reshape(sources * slots, width)
    gate = jnp.dot(flat_rows, w_gate[0], preferred_element_type=jnp.float32)
    upward = jnp.dot(flat_rows, w_up[0], preferred_element_type=jnp.float32)
    hidden = (jax.nn.silu(gate) * upward).astype(jnp.bfloat16)
    return hidden.reshape(sources, slots, hidden.shape[1])


def cross_gram(first, second):
    return lax.dot_general(
        first, second, (((0,), (0,)), ((), ())), preferred_element_type=jnp.float32
    )


def gram_of(hidden):
    middle = hidden.shape[1] // 2
    left_part = hidden[:, :middle]
    right_part = hidden[:, middle:]
    upper_left = cross_gram(left_part, left_part)
    upper_right = cross_gram(left_part, right_part)
    lower_right = cross_gram(right_part, right_part)
    top_band = jnp.concatenate([upper_left, upper_right], axis=1)
    bottom_band = jnp.concatenate([upper_right.T, lower_right], axis=1)
    return jnp.concatenate([top_band, bottom_band], axis=0)


def local(tokens, expert_ids, w_gate, w_up, down_error):
    across = lax.axis_size("gx")
    within = lax.axis_size("gy")
    experts = across * within
    tok_count, top_count = expert_ids.shape
    width = tokens.shape[1]
    assigned = tok_count * top_count
    capacity = 3 * assigned // experts
    flat_ids = expert_ids.reshape(assigned)
    onehot = (flat_ids[:, None] == jnp.arange(experts, dtype=jnp.int32)[None, :]).astype(
        jnp.bfloat16
    )
    positions = jnp.arange(assigned, dtype=jnp.int32)
    lower = (positions[:, None] >= positions[None, :]).astype(jnp.bfloat16)
    running = jnp.dot(lower, onehot, preferred_element_type=jnp.float32)
    slot_of = (jnp.sum(running * onehot, axis=1) - 1.0).astype(jnp.int32)
    target = flat_ids * capacity + slot_of
    picked = tokens[positions // top_count]
    outgoing = jnp.zeros((experts * capacity, width), jnp.bfloat16).at[target].set(picked)
    tallies = jnp.sum(onehot.astype(jnp.float32), axis=0)
    loads = lax.psum_scatter(tallies, ("gx", "gy"), scatter_dimension=0, tiled=True)
    hidden = hidden_rows(
        lax.all_to_all(
            outgoing.reshape(experts, capacity, width),
            ("gx", "gy"),
            split_axis=0,
            concat_axis=0,
            tiled=True,
        ),
        w_gate,
        w_up,
    )
    hidden = hidden.reshape(experts * capacity, hidden.shape[2])
    gram = gram_of(hidden)
    mean_gram = gram / loads[0]
    product = jnp.dot(
        mean_gram,
        down_error[0],
        preferred_element_type=jnp.float32,
        precision=lax.Precision.HIGHEST,
    )
    return product[None]


def solution(mesh):
    small = mesh.shape["gx"] == 8 and mesh.shape["gy"] == 4
    return jax.shard_map(
        fused_local if small else local,
        mesh=mesh,
        in_specs=(
            P(("gx", "gy"), None),
            P(("gx", "gy"), None),
            P(("gx", "gy"), None, None),
            P(("gx", "gy"), None, None),
            P(("gx", "gy"), None, None),
        ),
        out_specs=P(("gx", "gy"), None, None),
        check_vma=False,
    )
```
